32 devices in a mesh: fsdp: 4 (over z), tp: 4 (over y, core), sect: 2 (over x).
Axes of the slice: x: 2, y: 2, z: 4, core: 2. Of those that a mesh axis runs over, the one named last changes fastest.
Arguments:
- hidden: bfloat16 [4096, 8192], P('fsdp', 'sect'), may hold values from -6 to 6
- kv_weight: bfloat16 [8192, 2048], P(('sect', 'fsdp'), 'tp'), may hold values from -0.0625 to 0.0625
- readout: float32 [2048], P(('tp', 'sect')), may hold values from -0.125 to 0.125
- lengths: int32 [4, 4], P('fsdp'), may hold values from 1 to 512, as said below
- prompt_mask: int32 [4096], P('fsdp'), may hold values from 0 to 1, as said below
- group_ids: int32 [16], P('fsdp'), may hold values from 0 to 1
Outputs:
- keys_values: bfloat16 [4096, 2048], P('fsdp', ('tp', 'sect'))
- advantages: float32 [16], P('fsdp')
The draws below stay inside these ranges and needn't reach their ends.
Inputs may be any that keep to these rules, and one draw needn't show every extreme that they name: `lengths`: each row sums to 1024; some entry of each row equals 512. `prompt_mask`: within each sequence the zeros come before the ones; at each index of fsdp exactly one sequence has no ones.
All inputs are finite; a program needn't handle non-finite values.
Results may differ from the reference program's by a relative error of at most 0.00045.
Values may be sent and summed in bfloat16 or wider, within the bound.
A program may use at most 64 MiB of HBM per device.

```python
import jax
import jax.numpy as jnp
from jax import lax

D = 8192
KVW = 2048
TOK_DEV = 1024
SEQ_DEV = 4
MOST = 512
TOKENS = 4096
SEQS = 16
GROUPS = 2
N_FSDP = 4


def make_layout(key):
    layout_key = jax.random.fold_in(key, 7321)
    row_keys = jax.random.split(layout_key, N_FSDP)

    def one_row(row_key):
        perm_key, where_key, blank_key, prompt_key = jax.random.split(row_key, 4)
        remain = TOK_DEV - MOST
        cut_points = jnp.sort(jax.random.permutation(perm_key, remain - 1)[:SEQ_DEV - 2] + 1).astype(jnp.int32)
        borders = jnp.concatenate([jnp.zeros((1,), jnp.int32), cut_points, jnp.full((1,), remain, jnp.int32)])
        pieces = borders[1:] - borders[:-1]
        longest = jax.random.randint(where_key, (), 0, SEQ_DEV)
        slot_ids = jnp.arange(SEQ_DEV, dtype=jnp.int32)
        source = jnp.clip(jnp.where(slot_ids < longest, slot_ids, slot_ids - 1), 0, SEQ_DEV - 2)
        row_len = jnp.where(slot_ids == longest, MOST, pieces[source]).astype(jnp.int32)
        blank_seq = (longest + 1 + jax.random.randint(blank_key, (), 0, SEQ_DEV - 1)) % SEQ_DEV
        prompt = jax.random.randint(prompt_key, (SEQ_DEV,), 0, row_len).astype(jnp.int32)
        prompt = jnp.where(slot_ids == blank_seq, row_len, prompt)
        finish = jnp.cumsum(row_len).astype(jnp.int32)
        starts = finish - row_len
        answer = starts + prompt
        places = jnp.arange(TOK_DEV, dtype=jnp.int32)
        inside = (places[None, :] >= answer[:, None]) & (places[None, :] < finish[:, None])
        row_mask = jnp.sum(inside.astype(jnp.int32), axis=0).astype(jnp.int32)
        return (row_len, row_mask)
    all_lengths, all_masks = jax.vmap(one_row)(row_keys)
    return (all_lengths, all_masks.reshape(TOK_DEV * N_FSDP))


def draw_lengths(key, part):
    return make_layout(key)[0]


def draw_prompt_mask(key, part):
    return make_layout(key)[1]


def set_ends(drawn, stream_key, low, high):
    extent = drawn.shape
    spot = [jax.random.randint(jax.random.fold_in(stream_key, axis), (), 0, extent[axis]) for axis in range(len(extent))]
    drawn = drawn.at[tuple(spot)].set(low)
    longest = extent.index(max(extent))
    spot[longest] = (spot[longest] + 1) % extent[longest]
    return drawn.at[tuple(spot)].set(high)


def level_of(rng, extent, cuts, least, largest):
    gain, own = 1.0, jax.random.fold_in(rng, 6)
    for axis_at, parts in cuts:
        heights = jnp.exp(jax.random.uniform(jax.random.fold_in(own, axis_at), (parts,), jnp.float32, least / len(cuts), largest / len(cuts)))
        gain = gain * jnp.repeat(heights, extent[axis_at] // parts).reshape([-1 if axis == axis_at else 1 for axis in range(len(extent))])
    return gain


def bell_draw(rng, extent, spread, limit, cuts=(), kind=jnp.bfloat16):
    level = level_of(rng, extent, cuts, -0.22, 0.18) if cuts else 1.0
    result = jax.random.normal(rng, extent, jnp.float32) * spread * level
    return jnp.minimum(jnp.maximum(result, -limit), limit).astype(kind)


def setup_inputs(seed: int = 0) -> dict:
    splits = jax.random.split(jax.random.key(seed), 7)
    hidden = bell_draw(splits[0], (TOKENS, D), 1.0, 6.0, ((0, 4), (1, 2)))
    kv_weight = bell_draw(splits[1], (D, KVW), D ** -0.5, 0.0625, ((0, 8), (1, 4)))
    readout = bell_draw(splits[2], (KVW,), KVW ** -0.5, 0.125, ((0, 8),), jnp.float32)
    lengths = draw_lengths(jax.random.fold_in(splits[6], 71), 0)
    prompt_mask = draw_prompt_mask(jax.random.fold_in(splits[6], 71), 0)
    group_ids = set_ends(jax.random.randint(splits[5], (SEQS,), 0, GROUPS), jax.random.fold_in(splits[5], 1), 0, GROUPS - 1).astype(jnp.int32)
    return dict(hidden=hidden, kv_weight=kv_weight, readout=readout, lengths=lengths, prompt_mask=prompt_mask, group_ids=group_ids)


def reference(hidden, kv_weight, readout, lengths, prompt_mask, group_ids):
    proj = jnp.dot(hidden, kv_weight, preferred_element_type=jnp.float32)
    keys_values = proj.astype(jnp.bfloat16)
    token_score = jnp.dot(proj, readout, precision=lax.Precision.HIGHEST)
    maskf = prompt_mask.astype(jnp.float32)
    masked = (token_score * maskf).reshape(N_FSDP, TOK_DEV)
    maskr = maskf.reshape(N_FSDP, TOK_DEV)
    ends = jnp.cumsum(lengths, axis=1).astype(jnp.int32)
    starts = ends - lengths
    places = jnp.arange(TOK_DEV, dtype=jnp.int32)
    member = ((places[None, None, :] >= starts[:, :, None]) & (places[None, None, :] < ends[:, :, None])).astype(jnp.float32)
    seq_sum = lax.optimization_barrier(jnp.sum(member * masked[:, None, :], axis=2)).reshape(SEQS)
    count = lax.optimization_barrier(jnp.sum(member * maskr[:, None, :], axis=2)).reshape(SEQS)
    reward = seq_sum / jnp.sqrt(jnp.maximum(count, 1.0))
    onehot = (group_ids[:, None] == jnp.arange(GROUPS, dtype=jnp.int32)[None, :]).astype(jnp.float32)
    sizes = lax.optimization_barrier(jnp.sum(onehot, axis=0))
    mean_g = lax.optimization_barrier(jnp.sum(onehot * reward[:, None], axis=0)) / jnp.maximum(sizes, 1.0)
    mine = lax.optimization_barrier(jnp.sum(onehot * mean_g[None, :], axis=1))
    var_g = lax.optimization_barrier(jnp.sum(onehot * ((reward - mine) ** 2)[:, None], axis=0)) / jnp.maximum(sizes, 1.0)
    myvar = lax.optimization_barrier(jnp.sum(onehot * var_g[None, :], axis=1))
    advantages = (reward - mine) / jnp.sqrt(myvar + 1.0)
    return (keys_values, advantages)
```

```python
import functools

import jax
import jax.numpy as jnp
from jax import lax
from jax.experimental import pallas as pl
from jax.experimental.pallas import tpu as pltpu
from jax.sharding import PartitionSpec as P

MESH = pl.DeviceIdType.MESH


def kernel(
    n, nt, ns, parts, tile,
    hid_any, w_any, ro_ref, mask_ref, len_ref, gid_ref,
    kv_ref, adv_ref,
    hid, wbuf, acc, precv, member, sbuf, zbuf,
    hid_sem, own_sem, wsend, wrecv, xsend, xrecv, ssend, srecv, zsend, zrecv,
):
    f, t, s = lax.axis_index("fsdp"), lax.axis_index("tp"), lax.axis_index("sect")
    plane = nt * ns
    me = t * ns + s
    rows, width = w_any.shape
    cw = width // 2
    piece = rows // parts
    by_piece = piece % 128 == 0
    tok = hid.shape[0]

    def plane_id(k):
        other = lax.rem(me + k, plane)
        return {"tp": lax.div(other, ns), "sect": lax.rem(other, ns)}

    def line_id(k):
        return {"fsdp": lax.rem(f + k, n)}

    def cols(c):
        side = s if c else 1 - s
        return pl.ds(pl.multiple_of(side * cw, cw), cw)

    def depth_at(j, r):
        return pl.ds(pl.multiple_of(j * rows + r * piece, piece), piece)

    def own_rows(c, r):
        return w_any.at[r * piece:(r + 1) * piece, cols(c)]

    def w_copy(c, j, r, step, own):
        place = wbuf.at[c, depth_at(j, r), :]
        return pltpu.make_async_remote_copy(
            src_ref=own_rows(c, r) if own else place,
            dst_ref=place,
            send_sem=wsend.at[0 if step > 0 else 1, c, r, j],
            recv_sem=wrecv.at[c, r, j],
            device_id={"fsdp": f + step},
            device_id_type=MESH,
        )

    def x_copy():
        return pltpu.make_async_remote_copy(
            src_ref=acc.at[0],
            dst_ref=precv,
            send_sem=xsend,
            recv_sem=xrecv,
            device_id={"sect": 1 - s},
            device_id_type=MESH,
        )

    def s_copy(k, slot):
        return pltpu.make_async_remote_copy(
            src_ref=sbuf.at[slot],
            dst_ref=sbuf.at[slot],
            send_sem=ssend.at[k],
            recv_sem=srecv.at[slot],
            device_id=plane_id(k),
            device_id_type=MESH,
        )

    def z_copy(k, slot):
        return pltpu.make_async_remote_copy(
            src_ref=zbuf.at[slot],
            dst_ref=zbuf.at[slot],
            send_sem=zsend.at[k],
            recv_sem=zrecv.at[slot],
            device_id=line_id(k),
            device_id_type=MESH,
        )

    def each(low, high, body):
        def step(i, carry):
            body(i)
            return carry

        lax.fori_loop(low, high, step, 0)

    barrier = pltpu.get_barrier_semaphore()
    each(1, n, lambda k: pl.semaphore_signal(
        barrier, inc=1, device_id=line_id(k), device_id_type=MESH))
    each(1, plane, lambda k: pl.semaphore_signal(
        barrier, inc=1, device_id=plane_id(k), device_id_type=MESH))

    def own_copy(c, r):
        return pltpu.make_async_copy(
            own_rows(c, r), wbuf.at[c, depth_at(f, r), :], own_sem.at[c, r])

    def send_own(c, step):
        for r in range(parts):
            w_copy(c, f, r, step, True).start()

    pl.semaphore_wait(barrier, n - 1 + plane - 1)

    @pl.when(f < n - 1)
    def _():
        send_own(0, 1)

    @pl.when(f > 0)
    def _():
        send_own(0, -1)

    @pl.when(f == 0)
    def _():
        send_own(1, 1)

    @pl.when(f == n - 1)
    def _():
        send_own(1, -1)

    hid_copy = pltpu.make_async_copy(hid_any, hid, hid_sem)
    for c in range(2):
        for r in range(parts):
            own_copy(c, r).start()
    hid_copy.start()

    place = lax.broadcasted_iota(jnp.int32, (8, tok), 1)
    seq = lax.broadcasted_iota(jnp.int32, (8, tok), 0)
    inside = jnp.zeros((8, tok), jnp.bool_)
    start = jnp.int32(0)
    n_seq = len_ref.shape[1]
    for j in range(n_seq):
        finish = start + len_ref[0, j]
        inside = inside | ((seq == j) & (place >= start) & (place < finish))
        start = finish
    member[...] = inside.astype(jnp.float32) * mask_ref[...].astype(jnp.float32)

    def add(c, depth, first):
        def product(i, carry):
            at = pl.ds(pl.multiple_of(i * tile, tile), tile)
            part = jnp.dot(
                hid[at, depth], wbuf[c, depth, :], preferred_element_type=jnp.float32)
            acc[c, at, :] = part if first else acc[c, at, :] + part
            return carry

        lax.fori_loop(0, tok // tile, product, 0)

    def arrive(c, j, r, step):
        w_copy(c, j, r, -step, False).wait_recv()

        @pl.when((f + step >= 0) & (f + step < n))
        def _():
            w_copy(c, j, r, step, False).start()

        if by_piece:
            add(c, depth_at(j, r), False)

    for c in range(2):
        for r in range(parts):
            own_copy(c, r).wait()
        if c == 0:
            hid_copy.wait()
        if by_piece:
            add(c, pl.ds(pl.multiple_of(f * rows, rows), rows), True)

        def visit(d, c=c):
            left, right = f - d, f + d
            for r in range(parts):
                @pl.when(left >= 0)
                def _():
                    arrive(c, left, r, 1)

                @pl.when(right < n)
                def _():
                    arrive(c, right, r, -1)

            if c == 0:
                @pl.when((d == f) & (f < n - 1))
                def _():
                    send_own(1, 1)

                @pl.when((d == n - 1 - f) & (f > 0))
                def _():
                    send_own(1, -1)

        each(1, n, visit)
        if not by_piece:
            add(c, slice(None), True)
        if c == 0:
            x_copy().start()

    x_copy().wait_recv()

    def finish_rows(i, carry):
        at = pl.ds(pl.multiple_of(i * tile, tile), tile)
        projected = acc[1, at, :] + precv[at, :]
        kv_ref[at, :] = projected.astype(jnp.bfloat16)
        chosen = member[:, at].astype(jnp.bfloat16)
        rest = projected
        for _ in range(3):
            digits = rest.astype(jnp.bfloat16)
            carry += jnp.dot(chosen, digits, preferred_element_type=jnp.float32)
            rest = rest - digits.astype(jnp.float32)
        return carry

    total = lax.fori_loop(
        0, tok // tile, finish_rows, jnp.zeros((8, cw), jnp.float32)) * ro_ref[...]
    sbuf[me] = total
    each(1, plane, lambda k: s_copy(k, me).start())
    count = jnp.sum(member[...], axis=1, keepdims=True)
    each(1, plane, lambda k: s_copy(k, lax.rem(me + k, plane)).wait_recv())
    seq_sum = jnp.sum(jnp.sum(sbuf[...], axis=0), axis=1, keepdims=True)
    reward = seq_sum / jnp.sqrt(jnp.maximum(count, 1.0))

    row = lax.broadcasted_iota(jnp.int32, (8, 128), 0)
    lane = lax.broadcasted_iota(jnp.int32, (8, 128), 1)
    row_gid = jnp.full((8, 128), -1, jnp.int32)
    lane_gid = jnp.full((8, 128), -2, jnp.int32)
    for j in range(n_seq):
        row_gid = jnp.where(row == j, gid_ref[j], row_gid)
        lane_gid = jnp.where(lane == j, gid_ref[j], lane_gid)
    reward = jnp.broadcast_to(reward, (8, 128))
    zbuf[f, 0] = reward
    zbuf[f, 1] = row_gid.astype(jnp.float32)
    each(1, n, lambda k: z_copy(k, f).start())
    mine = jnp.sum(jnp.where(row == lane, reward, 0.0), axis=0, keepdims=True)
    each(1, n, lambda k: z_copy(k, lax.rem(f + k, n)).wait_recv())
    same = (zbuf[:, 1] == lane_gid.astype(jnp.float32)[None]).astype(jnp.float32)
    rewards = zbuf[:, 0]

    def over(value):
        return jnp.sum(jnp.sum(value, axis=0), axis=0, keepdims=True)

    size = jnp.maximum(over(same), 1.0)
    mean = over(same * rewards) / size
    var = over(same * (rewards - mean[None]) ** 2) / size
    adv_ref[...] = ((mine - mean) / jnp.sqrt(var + 1.0))[:, :n_seq]

    each(1, plane, lambda k: s_copy(k, me).wait_send())
    each(1, n, lambda k: z_copy(k, f).wait_send())
    x_copy().wait_send()
    for c in range(2):
        def sent(j, c=c):
            for r in range(parts):
                @pl.when((j <= f) & (f < n - 1))
                def _():
                    w_copy(c, j, r, 1, False).wait_send()

                @pl.when((j >= f) & (f > 0))
                def _():
                    w_copy(c, j, r, -1, False).wait_send()

        each(0, n, sent)


def line_kernel(
    nt, ns, parts, tile,
    hid_any, w_any, ro_ref, mask_ref, len_ref, gid_ref,
    kv_ref, adv_ref,
    hid, wbuf, acc, precv, member, gsum, robuf, vbuf, sbuf, zbuf,
    hid_sem, own_sem, wsend, wrecv, xsend, xrecv, rsend, rrecv,
    vsend, vrecv, ssend, srecv, zsend, zrecv,
):
    n = 4
    f, t, s = lax.axis_index("fsdp"), lax.axis_index("tp"), lax.axis_index("sect")
    plane = nt * ns
    me = t * ns + s
    rows, width = w_any.shape
    cw = width // 2
    piece = rows // parts
    tok, depth = hid.shape
    tiles = tok // tile
    inward = jnp.where(f < 2, 1, -1)
    outer = (f == 0) | (f == n - 1)
    inner = (f == 1) | (f == n - 2)

    def plane_id(k):
        other = lax.rem(me + k, plane)
        return {"tp": lax.div(other, ns), "sect": lax.rem(other, ns)}

    def line_id(k):
        return {"fsdp": lax.rem(f + k, n)}

    def cols(c):
        side = s if c else 1 - s
        return pl.ds(pl.multiple_of(side * cw, cw), cw)

    def depth_at(j, r):
        return pl.ds(pl.multiple_of(j * rows + r * piece, piece), piece)

    def block_at(j):
        return pl.ds(pl.multiple_of(j * rows, rows), rows)

    def remote(src, dst, send, recv, device):
        return pltpu.make_async_remote_copy(
            src_ref=src, dst_ref=dst, send_sem=send, recv_sem=recv,
            device_id=device, device_id_type=MESH)

    def w_copy(c, j, r, step, own=False):
        place = wbuf.at[c, depth_at(j, r), :]
        src = w_any.at[r * piece:(r + 1) * piece, cols(c)] if own else place
        toward = 0 if step is inward else 1
        return remote(src, place, wsend.at[toward, c, r, j], wrecv.at[c, r, j], {"fsdp": f + step})

    def x_copy(i):
        at = pl.ds(pl.multiple_of(i * tile, tile), tile)
        return remote(acc.at[0, at], precv.at[at], xsend.at[i], xrecv.at[i], {"sect": 1 - s})

    def r_copy():
        return remote(ro_ref, robuf, rsend, rrecv, {"sect": 1 - s})

    def v_copy(k, slot):
        return remote(vbuf.at[slot], vbuf.at[slot], vsend.at[k], vrecv.at[slot], line_id(k))

    def s_copy(k, slot):
        return remote(sbuf.at[slot], sbuf.at[slot], ssend.at[k], srecv.at[slot], plane_id(k))

    def z_copy(k, slot):
        return remote(zbuf.at[slot], zbuf.at[slot], zsend.at[k], zrecv.at[slot], line_id(k))

    def own_copy(c):
        return pltpu.make_async_copy(
            w_any.at[:, cols(c)], wbuf.at[c, block_at(f), :], own_sem.at[c])

    def each(low, high, body):
        def step(i, carry):
            body(i)
            return carry

        lax.fori_loop(low, high, step, 0)

    outward = -inward

    def send_own(c, r, step):
        w_copy(c, f, r, step, own=True).start()

    def take(c, j, r, step=None):
        w_copy(c, j, r, outward).wait_recv()
        if step is not None:
            w_copy(c, j, r, step).start()

    barrier = pltpu.get_barrier_semaphore()
    each(1, n, lambda k: pl.semaphore_signal(
        barrier, inc=1, device_id=line_id(k), device_id_type=MESH))
    each(1, plane, lambda k: pl.semaphore_signal(
        barrier, inc=1, device_id=plane_id(k), device_id_type=MESH))
    hid_copy = pltpu.make_async_copy(hid_any, hid, hid_sem)
    for c in (1, 0):
        own_copy(c).start()
    hid_copy.start()
    pl.semaphore_wait(barrier, n - 1 + plane - 1)

    for r in range(parts):
        send_own(0, r, inward)

        @pl.when(inner)
        def _():
            send_own(0, r, outward)
    r_copy().start()

    place = lax.broadcasted_iota(jnp.int32, (8, tok), 1)
    seq = lax.broadcasted_iota(jnp.int32, (8, tok), 0)
    inside = jnp.zeros((8, tok), jnp.bool_)
    start = jnp.int32(0)
    n_seq = len_ref.shape[1]
    for j in range(n_seq):
        finish = start + len_ref[0, j]
        inside = inside | ((seq == j) & (place >= start) & (place < finish))
        start = finish
    member[...] = inside.astype(jnp.float32) * mask_ref[...].astype(jnp.float32)

    def weigh():
        line = lax.broadcasted_iota(jnp.int32, (8, cw), 0)
        total = jnp.zeros((8, rows), jnp.float32)
        for c in (1, 0):
            if c == 0:
                r_copy().wait_recv()
            own_copy(c).wait()
            rest = jnp.broadcast_to((ro_ref if c else robuf)[...], (8, cw))
            digits = jnp.zeros((8, cw), jnp.float32)
            for k in range(3):
                digit = rest.astype(jnp.bfloat16).astype(jnp.float32)
                digits = jnp.where(line == k, digit, digits)
                rest = rest - digit
            total += lax.dot_general(
                digits.astype(jnp.bfloat16), wbuf[c, block_at(f), :],
                (((1,), (1,)), ((), ())), preferred_element_type=jnp.float32)
        total = jnp.sum(total, axis=0, keepdims=True)
        for i in range(rows // 128):
            vbuf[f, i:i + 1, :] = total[:, i * 128:(i + 1) * 128]
        for k in range(1, n):
            v_copy(k, f).start()

    def gather_tokens():
        hid_copy.wait()
        chosen = member[...].astype(jnp.bfloat16)
        step = 512 if depth % 512 == 0 else 128

        def part(i):
            at = pl.ds(pl.multiple_of(i * step, step), step)
            gsum[:, at] = jnp.dot(chosen, hid[:, at], preferred_element_type=jnp.float32)

        each(0, depth // step, part)

    def score():
        for k in range(1, n):
            v_copy(k, lax.rem(f + k, n)).wait_recv()
        total = jnp.zeros((8, 128), jnp.float32)
        for j in range(n):
            for i in range(rows // 128):
                at = j * rows + i * 128
                total += gsum[:, at:at + 128] * vbuf[j, i:i + 1, :]
        sbuf[me] = jnp.broadcast_to(jnp.sum(total, axis=1, keepdims=True), (8, 128))
        each(1, plane, lambda k: s_copy(k, me).start())

    row = lax.broadcasted_iota(jnp.int32, (8, 128), 0)
    lane = lax.broadcasted_iota(jnp.int32, (8, 128), 1)

    def reward():
        count = jnp.sum(member[...], axis=1, keepdims=True)
        each(1, plane, lambda k: s_copy(k, lax.rem(me + k, plane)).wait_recv())
        seq_sum = jnp.sum(sbuf[...], axis=0)
        row_gid = jnp.full((8, 128), -1, jnp.int32)
        for j in range(n_seq):
            row_gid = jnp.where(row == j, gid_ref[j], row_gid)
        zbuf[f, 0] = seq_sum / jnp.sqrt(jnp.maximum(count, 1.0))
        zbuf[f, 1] = row_gid.astype(jnp.float32)
        each(1, n, lambda k: z_copy(k, f).start())

    def advantage():
        each(1, n, lambda k: z_copy(k, lax.rem(f + k, n)).wait_recv())
        lane_gid = jnp.full((8, 128), -2, jnp.int32)
        for j in range(n_seq):
            lane_gid = jnp.where(lane == j, gid_ref[j], lane_gid)
        mine = jnp.sum(jnp.where(row == lane, zbuf[f, 0], 0.0), axis=0, keepdims=True)
        same = (zbuf[:, 1] == lane_gid.astype(jnp.float32)[None]).astype(jnp.float32)
        rewards = zbuf[:, 0]

        def over(value):
            return jnp.sum(jnp.sum(value, axis=0), axis=0, keepdims=True)

        size = jnp.maximum(over(same), 1.0)
        mean = over(same * rewards) / size
        var = over(same * (rewards - mean[None]) ** 2) / size
        adv_ref[...] = ((mine - mean) / jnp.sqrt(var + 1.0))[:, :n_seq]

    def add(c, at_depth, first=False, send=False):
        def product(i):
            at = pl.ds(pl.multiple_of(i * tile, tile), tile)
            part = jnp.dot(
                hid[at, at_depth], wbuf[c, at_depth, :], preferred_element_type=jnp.float32)
            acc[c, at, :] = part if first else acc[c, at, :] + part
            if send:
                x_copy(i).start()

        each(0, tiles, product)

    def finish(at_depth):
        def product(i):
            at = pl.ds(pl.multiple_of(i * tile, tile), tile)
            part = jnp.dot(
                hid[at, at_depth], wbuf[1, at_depth, :], preferred_element_type=jnp.float32)
            kv_ref[at, :] = (acc[1, at, :] + precv[at, :] + part).astype(jnp.bfloat16)

        each(0, tiles, product)

    weigh()

    @pl.when(outer)
    def _():
        mid, far, end = f + inward, f + 2 * inward, f + 3 * inward
        for r in range(parts):
            send_own(1, r, inward)
        gather_tokens()
        for c in range(2):
            add(c, block_at(f), first=True)
        for r in range(parts):
            take(0, mid, r)
        add(0, block_at(mid))
        score()
        for r in range(parts):
            take(0, far, r)
        add(0, block_at(far))
        reward()
        for r in range(parts):
            take(0, end, r)
        add(0, block_at(end), send=True)
        for r in range(parts):
            take(1, mid, r)
        add(1, block_at(mid))
        advantage()
        for r in range(parts):
            take(1, far, r)
        add(1, block_at(far))
        for r in range(parts - 1):
            take(1, end, r)
            add(1, depth_at(end, r))
        each(0, tiles, lambda i: x_copy(i).wait_recv())
        take(1, end, parts - 1)
        finish(depth_at(end, parts - 1))

    @pl.when(inner)
    def _():
        mine, edge, far, end = f, f + outward, f + inward, f + 2 * inward
        send_own(1, 0, outward)
        for r in range(parts):
            take(0, edge, r, inward)
        for r in range(parts):
            send_own(1, r, inward)
        for r in range(parts):
            take(0, far, r, outward)
        gather_tokens()
        add(0, block_at(mine), first=True)
        for r in range(parts):
            take(0, end, r, outward)
        for r in range(1, parts):
            send_own(1, r, outward)
        score()
        for r in range(parts):
            take(1, edge, r, inward)
        add(0, block_at(edge))
        add(0, block_at(far))
        reward()
        add(0, block_at(end), send=True)
        for r in range(parts):
            take(1, far, r, outward)
        add(1, block_at(mine), first=True)
        add(1, block_at(edge))
        for r in range(parts):
            take(1, end, r, outward)
        add(1, block_at(far))
        advantage()
        each(0, tiles, lambda i: x_copy(i).wait_recv())
        finish(block_at(end))

    each(0, tiles, lambda i: x_copy(i).wait_send())
    r_copy().wait_send()
    for k in range(1, n):
        v_copy(k, f).wait_send()
    each(1, plane, lambda k: s_copy(k, me).wait_send())
    each(1, n, lambda k: z_copy(k, f).wait_send())
    for c in range(2):
        for r in range(parts):
            w_copy(c, f, r, inward).wait_send()

            @pl.when(inner)
            def _():
                w_copy(c, f, r, outward).wait_send()
                w_copy(c, f + outward, r, inward).wait_send()
                w_copy(c, f + inward, r, outward).wait_send()
                w_copy(c, f + 2 * inward, r, outward).wait_send()


def solution(mesh):
    n, nt, ns = mesh.shape["fsdp"], mesh.shape["tp"], mesh.shape["sect"]

    def local(hidden, kv_weight, readout, lengths, prompt_mask, group_ids):
        tok, depth = hidden.shape
        rows, width = kv_weight.shape
        parts = max(1, min(2, rows // 256))
        cw = width // 2
        plane = nt * ns
        n_seq = lengths.shape[1]
        tile = min(256, tok)
        in_line = n == 4 and ns == 2 and rows % 1024 == 0 and cw % 128 == 0 and tok % tile == 0
        dma = pltpu.SemaphoreType.DMA
        vmem, smem, anywhere = (
            pl.BlockSpec(memory_space=pltpu.VMEM),
            pl.BlockSpec(memory_space=pltpu.SMEM),
            pl.BlockSpec(memory_space=pl.ANY),
        )
        if in_line:
            body = functools.partial(line_kernel, nt, ns, parts, tile)
            tiles = tok // tile
            scratch = [
                pltpu.VMEM((tok, depth), jnp.bfloat16),
                pltpu.VMEM((2, depth, cw), jnp.bfloat16),
                pltpu.VMEM((2, tok, cw), jnp.float32),
                pltpu.VMEM((tok, cw), jnp.float32),
                pltpu.VMEM((8, tok), jnp.float32),
                pltpu.VMEM((8, depth), jnp.float32),
                pltpu.VMEM((1, cw), jnp.float32),
                pltpu.VMEM((n, rows // 128, 128), jnp.float32),
                pltpu.VMEM((plane, 8, 128), jnp.float32),
                pltpu.VMEM((n, 2, 8, 128), jnp.float32),
                dma, dma((2,)),
                dma((2, 2, parts, n)), dma((2, parts, n)),
                dma((tiles,)), dma((tiles,)),
                dma, dma,
                dma((n,)), dma((n,)),
                dma((plane,)), dma((plane,)),
                dma((n,)), dma((n,)),
            ]
        else:
            body = functools.partial(kernel, n, nt, ns, parts, tile)
            scratch = [
                pltpu.VMEM((tok, depth), jnp.bfloat16),
                pltpu.VMEM((2, depth, cw), jnp.bfloat16),
                pltpu.VMEM((2, tok, cw), jnp.float32),
                pltpu.VMEM((tok, cw), jnp.float32),
                pltpu.VMEM((8, tok), jnp.float32),
                pltpu.VMEM((plane, 8, cw), jnp.float32),
                pltpu.VMEM((n, 2, 8, 128), jnp.float32),
                dma, dma((2, parts)),
                dma((2, 2, parts, n)), dma((2, parts, n)),
                dma, dma,
                dma((plane,)), dma((plane,)),
                dma((n,)), dma((n,)),
            ]
        kv, adv = pl.pallas_call(
            body,
            out_shape=(
                pltpu.VMEM((tok, width // 2), jnp.bfloat16),
                pltpu.VMEM((1, n_seq), jnp.float32),
            ),
            in_specs=[anywhere, anywhere, vmem, vmem, smem, smem],
            out_specs=(vmem, vmem),
            scratch_shapes=scratch,
            compiler_params=pltpu.CompilerParams(collective_id=0, has_side_effects=True),
        )(hidden, kv_weight, readout[None, :], prompt_mask[None, :], lengths, group_ids)
        return kv, adv[0]

    return jax.shard_map(
        local,
        mesh=mesh,
        in_specs=(
            P("fsdp", "sect"),
            P(("sect", "fsdp"), "tp"),
            P(("tp", "sect")),
            P("fsdp", None),
            P("fsdp"),
            P("fsdp"),
        ),
        out_specs=(P("fsdp", ("tp", "sect")), P("fsdp")),
        check_vma=False,
    )
```

```python
import functools

import jax
import jax.numpy as jnp
from jax import lax
from jax.experimental import pallas as pl
from jax.experimental.pallas import tpu as pltpu
from jax.sharding import PartitionSpec as P

MESH = pl.DeviceIdType.MESH


def kernel(
    n, nt, ns, parts, tile,
    hid_any, w_any, ro_ref, mask_ref, len_ref, gid_ref,
    kv_ref, adv_ref,
    hid, wbuf, acc, precv, member, sbuf, zbuf,
    hid_sem, own_sem, wsend, wrecv, xsend, xrecv, ssend, srecv, zsend, zrecv,
):
    f, t, s = lax.axis_index("fsdp"), lax.axis_index("tp"), lax.axis_index("sect")
    plane = nt * ns
    me = t * ns + s
    rows, width = w_any.shape
    cw = width // 2
    piece = rows // parts
    by_piece = piece % 128 == 0
    tok = hid.shape[0]

    def plane_id(k):
        other = lax.rem(me + k, plane)
        return {"tp": lax.div(other, ns), "sect": lax.rem(other, ns)}

    def line_id(k):
        return {"fsdp": lax.rem(f + k, n)}

    def cols(c):
        side = s if c else 1 - s
        return pl.ds(pl.multiple_of(side * cw, cw), cw)

    def depth_at(j, r):
        return pl.ds(pl.multiple_of(j * rows + r * piece, piece), piece)

    def own_rows(c, r):
        return w_any.at[r * piece:(r + 1) * piece, cols(c)]

    def w_copy(c, j, r, step, own):
        place = wbuf.at[c, depth_at(j, r), :]
        return pltpu.make_async_remote_copy(
            src_ref=own_rows(c, r) if own else place,
            dst_ref=place,
            send_sem=wsend.at[0 if step > 0 else 1, c, r, j],
            recv_sem=wrecv.at[c, r, j],
            device_id={"fsdp": f + step},
            device_id_type=MESH,
        )

    def x_copy():
        return pltpu.make_async_remote_copy(
            src_ref=acc.at[0],
            dst_ref=precv,
            send_sem=xsend,
            recv_sem=xrecv,
            device_id={"sect": 1 - s},
            device_id_type=MESH,
        )

    def s_copy(k, slot):
        return pltpu.make_async_remote_copy(
            src_ref=sbuf.at[slot],
            dst_ref=sbuf.at[slot],
            send_sem=ssend.at[k],
            recv_sem=srecv.at[slot],
            device_id=plane_id(k),
            device_id_type=MESH,
        )

    def z_copy(k, slot):
        return pltpu.make_async_remote_copy(
            src_ref=zbuf.at[slot],
            dst_ref=zbuf.at[slot],
            send_sem=zsend.at[k],
            recv_sem=zrecv.at[slot],
            device_id=line_id(k),
            device_id_type=MESH,
        )

    def each(low, high, body):
        def step(i, carry):
            body(i)
            return carry

        lax.fori_loop(low, high, step, 0)

    barrier = pltpu.get_barrier_semaphore()
    each(1, n, lambda k: pl.semaphore_signal(
        barrier, inc=1, device_id=line_id(k), device_id_type=MESH))
    each(1, plane, lambda k: pl.semaphore_signal(
        barrier, inc=1, device_id=plane_id(k), device_id_type=MESH))

    def own_copy(c, r):
        return pltpu.make_async_copy(
            own_rows(c, r), wbuf.at[c, depth_at(f, r), :], own_sem.at[c, r])

    def send_own(c, step):
        for r in range(parts):
            w_copy(c, f, r, step, True).start()

    pl.semaphore_wait(barrier, n - 1 + plane - 1)

    @pl.when(f < n - 1)
    def _():
        send_own(0, 1)

    @pl.when(f > 0)
    def _():
        send_own(0, -1)

    @pl.when(f == 0)
    def _():
        send_own(1, 1)

    @pl.when(f == n - 1)
    def _():
        send_own(1, -1)

    hid_copy = pltpu.make_async_copy(hid_any, hid, hid_sem)
    for c in range(2):
        for r in range(parts):
            own_copy(c, r).start()
    hid_copy.start()

    place = lax.broadcasted_iota(jnp.int32, (8, tok), 1)
    seq = lax.broadcasted_iota(jnp.int32, (8, tok), 0)
    inside = jnp.zeros((8, tok), jnp.bool_)
    start = jnp.int32(0)
    n_seq = len_ref.shape[1]
    for j in range(n_seq):
        finish = start + len_ref[0, j]
        inside = inside | ((seq == j) & (place >= start) & (place < finish))
        start = finish
    member[...] = inside.astype(jnp.float32) * mask_ref[...].astype(jnp.float32)

    def add(c, depth, first):
        def product(i, carry):
            at = pl.ds(pl.multiple_of(i * tile, tile), tile)
            part = jnp.dot(
                hid[at, depth], wbuf[c, depth, :], preferred_element_type=jnp.float32)
            acc[c, at, :] = part if first else acc[c, at, :] + part
            return carry

        lax.fori_loop(0, tok // tile, product, 0)

    def arrive(c, j, r, step):
        w_copy(c, j, r, -step, False).wait_recv()

        @pl.when((f + step >= 0) & (f + step < n))
        def _():
            w_copy(c, j, r, step, False).start()

        if by_piece:
            add(c, depth_at(j, r), False)

    for c in range(2):
        for r in range(parts):
            own_copy(c, r).wait()
        if c == 0:
            hid_copy.wait()
        if by_piece:
            add(c, pl.ds(pl.multiple_of(f * rows, rows), rows), True)

        def visit(d, c=c):
            left, right = f - d, f + d
            for r in range(parts):
                @pl.when(left >= 0)
                def _():
                    arrive(c, left, r, 1)

                @pl.when(right < n)
                def _():
                    arrive(c, right, r, -1)

            if c == 0:
                @pl.when((d == f) & (f < n - 1))
                def _():
                    send_own(1, 1)

                @pl.when((d == n - 1 - f) & (f > 0))
                def _():
                    send_own(1, -1)

        each(1, n, visit)
        if not by_piece:
            add(c, slice(None), True)
        if c == 0:
            x_copy().start()

    x_copy().wait_recv()

    def finish_rows(i, carry):
        at = pl.ds(pl.multiple_of(i * tile, tile), tile)
        projected = acc[1, at, :] + precv[at, :]
        kv_ref[at, :] = projected.astype(jnp.bfloat16)
        chosen = member[:, at].astype(jnp.bfloat16)
        rest = projected
        for _ in range(3):
            digits = rest.astype(jnp.bfloat16)
            carry += jnp.dot(chosen, digits, preferred_element_type=jnp.float32)
            rest = rest - digits.astype(jnp.float32)
        return carry

    total = lax.fori_loop(
        0, tok // tile, finish_rows, jnp.zeros((8, cw), jnp.float32)) * ro_ref[...]
    sbuf[me] = total
    each(1, plane, lambda k: s_copy(k, me).start())
    count = jnp.sum(member[...], axis=1, keepdims=True)
    each(1, plane, lambda k: s_copy(k, lax.rem(me + k, plane)).wait_recv())
    seq_sum = jnp.sum(jnp.sum(sbuf[...], axis=0), axis=1, keepdims=True)
    reward = seq_sum / jnp.sqrt(jnp.maximum(count, 1.0))

    row = lax.broadcasted_iota(jnp.int32, (8, 128), 0)
    lane = lax.broadcasted_iota(jnp.int32, (8, 128), 1)
    row_gid = jnp.full((8, 128), -1, jnp.int32)
    lane_gid = jnp.full((8, 128), -2, jnp.int32)
    for j in range(n_seq):
        row_gid = jnp.where(row == j, gid_ref[j], row_gid)
        lane_gid = jnp.where(lane == j, gid_ref[j], lane_gid)
    reward = jnp.broadcast_to(reward, (8, 128))
    zbuf[f, 0] = reward
    zbuf[f, 1] = row_gid.astype(jnp.float32)
    each(1, n, lambda k: z_copy(k, f).start())
    mine = jnp.sum(jnp.where(row == lane, reward, 0.0), axis=0, keepdims=True)
    each(1, n, lambda k: z_copy(k, lax.rem(f + k, n)).wait_recv())
    same = (zbuf[:, 1] == lane_gid.astype(jnp.float32)[None]).astype(jnp.float32)
    rewards = zbuf[:, 0]

    def over(value):
        return jnp.sum(jnp.sum(value, axis=0), axis=0, keepdims=True)

    size = jnp.maximum(over(same), 1.0)
    mean = over(same * rewards) / size
    var = over(same * (rewards - mean[None]) ** 2) / size
    adv_ref[...] = ((mine - mean) / jnp.sqrt(var + 1.0))[:, :n_seq]

    each(1, plane, lambda k: s_copy(k, me).wait_send())
    each(1, n, lambda k: z_copy(k, f).wait_send())
    x_copy().wait_send()
    for c in range(2):
        def sent(j, c=c):
            for r in range(parts):
                @pl.when((j <= f) & (f < n - 1))
                def _():
                    w_copy(c, j, r, 1, False).wait_send()

                @pl.when((j >= f) & (f > 0))
                def _():
                    w_copy(c, j, r, -1, False).wait_send()

        each(0, n, sent)


def line_kernel(
    nt, ns, parts, tile,
    hid_any, w_any, ro_ref, mask_ref, len_ref, gid_ref,
    kv_ref, adv_ref,
    hid, wbuf, acc, precv, hbuf, racc, rx, rret, member, gsum, robuf, vbuf, sbuf, zbuf,
    hid_sem, own_sem, wsend, wrecv, xsend, xrecv, rsend, rrecv,
    vsend, vrecv, ssend, srecv, zsend, zrecv,
    hsend, hrecv, qsend, qrecv, bsend, brecv,
):
    n = 4
    f, t, s = lax.axis_index("fsdp"), lax.axis_index("tp"), lax.axis_index("sect")
    plane = nt * ns
    me = t * ns + s
    rows, width = w_any.shape
    cw = width // 2
    qw = cw // 2
    piece = rows // parts
    tok, depth = hid.shape
    tiles = tok // tile
    share = tile // nt
    inward = jnp.where(f < 2, 1, -1)
    outward = -inward
    outer = (f == 0) | (f == n - 1)
    inner = (f == 1) | (f == n - 2)
    near_at = jnp.where(f < 2, 0, 2 * rows)
    near = pl.ds(pl.multiple_of(near_at, rows), 2 * rows)
    far = pl.ds(pl.multiple_of(2 * rows - near_at, rows), 2 * rows)
    mate = lax.div(t, 2) * 2 + (1 - lax.rem(t, 2))
    across = lax.rem(t + 2, 4)
    cross = lax.rem(mate + 2, 4)

    def plane_id(k):
        other = lax.rem(me + k, plane)
        return {"tp": lax.div(other, ns), "sect": lax.rem(other, ns)}

    def line_id(k):
        return {"fsdp": lax.rem(f + k, n)}

    def cols(q):
        side = s if q >= 2 else 1 - s
        return pl.ds(pl.multiple_of(side * cw + (q % 2) * qw, qw), qw)

    def depth_at(j, r):
        return pl.ds(pl.multiple_of(j * rows + r * piece, piece), piece)

    def block_at(j):
        return pl.ds(pl.multiple_of(j * rows, rows), rows)

    def tile_at(i):
        return pl.ds(pl.multiple_of(i * tile, tile), tile)

    def share_at(i, p):
        return pl.ds(pl.multiple_of(i * tile + p * share, share), share)

    def remote(src, dst, send, recv, device):
        return pltpu.make_async_remote_copy(
            src_ref=src, dst_ref=dst, send_sem=send, recv_sem=recv,
            device_id=device, device_id_type=MESH)

    def w_copy(q, j, r, step, own=False):
        place = wbuf.at[q, depth_at(j, r), :]
        src = w_any.at[r * piece:(r + 1) * piece, cols(q)] if own else place
        toward = 0 if step is inward else 1
        return remote(src, place, wsend.at[toward, q, r, j], wrecv.at[q, r, j], {"fsdp": f + step})

    def x_copy(q, i):
        at = tile_at(i)
        return remote(acc.at[q, at], precv.at[q, at], xsend.at[q, i], xrecv.at[q, i], {"sect": 1 - s})

    def h_copy(i):
        at = share_at(i, t)
        return remote(hid.at[at, far], hbuf.at[at], hsend.at[0, i], hrecv.at[i, t], {"fsdp": f + inward})

    def h_spread(k, i):
        p = (t, t, across)[k]
        to = (mate, across, mate)[k]
        at = share_at(i, p)
        return remote(hbuf.at[at], hbuf.at[at], hsend.at[k, i], hrecv.at[i, p], {"tp": to})

    def h_recv(i, p):
        at = share_at(i, p)
        return remote(hbuf.at[at], hbuf.at[at], hsend.at[0, i], hrecv.at[i, p], {"tp": mate})

    def q_copy(i):
        at = tile_at(i)
        return remote(racc.at[0, at], rx.at[at], qsend.at[i], qrecv.at[i], {"sect": 1 - s})

    def b_copy(i):
        at = tile_at(i)
        return remote(racc.at[1, at], rret.at[at], bsend.at[i], brecv.at[i], {"fsdp": f + outward})

    def r_copy():
        return remote(ro_ref, robuf, rsend, rrecv, {"sect": 1 - s})

    def v_copy(k, slot):
        return remote(vbuf.at[slot], vbuf.at[slot], vsend.at[k], vrecv.at[slot], line_id(k))

    def s_copy(k, slot):
        return remote(sbuf.at[slot], sbuf.at[slot], ssend.at[k], srecv.at[slot], plane_id(k))

    def z_copy(k, slot):
        return remote(zbuf.at[slot], zbuf.at[slot], zsend.at[k], zrecv.at[slot], line_id(k))

    def own_copy(q):
        return pltpu.make_async_copy(
            w_any.at[:, cols(q)], wbuf.at[q, block_at(f), :], own_sem.at[q])

    def each(low, high, body):
        def step(i, carry):
            body(i)
            return carry

        lax.fori_loop(low, high, step, 0)

    def send_own(q, step):
        for r in range(parts):
            w_copy(q, f, r, step, own=True).start()

    def take(q, j, step=None):
        for r in range(parts):
            w_copy(q, j, r, outward).wait_recv()
            if step is not None:
                w_copy(q, j, r, step).start()

    barrier = pltpu.get_barrier_semaphore()
    each(1, n, lambda k: pl.semaphore_signal(
        barrier, inc=1, device_id=line_id(k), device_id_type=MESH))
    each(1, plane, lambda k: pl.semaphore_signal(
        barrier, inc=1, device_id=plane_id(k), device_id_type=MESH))
    for q in (2, 3, 0, 1):
        own_copy(q).start()
    hid_copy = pltpu.make_async_copy(hid_any, hid, hid_sem)
    hid_copy.start()
    pl.semaphore_wait(barrier, n - 1 + plane - 1)

    send_own(0, inward)

    @pl.when(inner)
    def _():
        send_own(0, outward)

    r_copy().start()

    place = lax.broadcasted_iota(jnp.int32, (8, tok), 1)
    seq = lax.broadcasted_iota(jnp.int32, (8, tok), 0)
    inside = jnp.zeros((8, tok), jnp.bool_)
    start = jnp.int32(0)
    n_seq = len_ref.shape[1]
    for j in range(n_seq):
        finish = start + len_ref[0, j]
        inside = inside | ((seq == j) & (place >= start) & (place < finish))
        start = finish
    member[...] = inside.astype(jnp.float32) * mask_ref[...].astype(jnp.float32)

    def weigh():
        line = lax.broadcasted_iota(jnp.int32, (8, qw), 0)
        total = jnp.zeros((8, rows), jnp.float32)
        for q in (2, 3, 0, 1):
            if q == 0:
                r_copy().wait_recv()
            own_copy(q).wait()
            values = (ro_ref if q >= 2 else robuf)[:, (q % 2) * qw:(q % 2 + 1) * qw]
            rest = jnp.broadcast_to(values, (8, qw))
            digits = jnp.zeros((8, qw), jnp.float32)
            for k in range(3):
                digit = rest.astype(jnp.bfloat16).astype(jnp.float32)
                digits = jnp.where(line == k, digit, digits)
                rest = rest - digit
            total += lax.dot_general(
                digits.astype(jnp.bfloat16), wbuf[q, block_at(f), :],
                (((1,), (1,)), ((), ())), preferred_element_type=jnp.float32)
        total = jnp.sum(total, axis=0, keepdims=True)
        for i in range(rows // 128):
            vbuf[f, i:i + 1, :] = total[:, i * 128:(i + 1) * 128]
        for k in range(1, n):
            v_copy(k, f).start()

    def gather_tokens():
        chosen = member[...].astype(jnp.bfloat16)
        step = 512 if depth % 512 == 0 else 128

        def part(i):
            at = pl.ds(pl.multiple_of(i * step, step), step)
            gsum[:, at] = jnp.dot(chosen, hid[:, at], preferred_element_type=jnp.float32)

        each(0, depth // step, part)

    def score():
        for k in range(1, n):
            v_copy(k, lax.rem(f + k, n)).wait_recv()
        total = jnp.zeros((8, 128), jnp.float32)
        for j in range(n):
            for i in range(rows // 128):
                at = j * rows + i * 128
                total += gsum[:, at:at + 128] * vbuf[j, i:i + 1, :]
        sbuf[me] = jnp.broadcast_to(jnp.sum(total, axis=1, keepdims=True), (8, 128))
        each(1, plane, lambda k: s_copy(k, me).start())

    row = lax.broadcasted_iota(jnp.int32, (8, 128), 0)
    lane = lax.broadcasted_iota(jnp.int32, (8, 128), 1)

    def reward():
        count = jnp.sum(member[...], axis=1, keepdims=True)
        each(1, plane, lambda k: s_copy(k, lax.rem(me + k, plane)).wait_recv())
        seq_sum = jnp.sum(sbuf[...], axis=0)
        row_gid = jnp.full((8, 128), -1, jnp.int32)
        for j in range(n_seq):
            row_gid = jnp.where(row == j, gid_ref[j], row_gid)
        zbuf[f, 0] = seq_sum / jnp.sqrt(jnp.maximum(count, 1.0))
        zbuf[f, 1] = row_gid.astype(jnp.float32)
        each(1, n, lambda k: z_copy(k, f).start())

    def advantage():
        each(1, n, lambda k: z_copy(k, lax.rem(f + k, n)).wait_recv())
        lane_gid = jnp.full((8, 128), -2, jnp.int32)
        for j in range(n_seq):
            lane_gid = jnp.where(lane == j, gid_ref[j], lane_gid)
        mine = jnp.sum(jnp.where(row == lane, zbuf[f, 0], 0.0), axis=0, keepdims=True)
        same = (zbuf[:, 1] == lane_gid.astype(jnp.float32)[None]).astype(jnp.float32)
        rewards = zbuf[:, 0]

        def over(value):
            return jnp.sum(jnp.sum(value, axis=0), axis=0, keepdims=True)

        size = jnp.maximum(over(same), 1.0)
        mean = over(same * rewards) / size
        var = over(same * (rewards - mean[None]) ** 2) / size
        adv_ref[...] = ((mine - mean) / jnp.sqrt(var + 1.0))[:, :n_seq]

    def add(q, at_depth, first=False, send=False, low=0, high=tiles):
        def product(i):
            at = tile_at(i)
            part = jnp.dot(
                hid[at, at_depth], wbuf[q, at_depth, :], preferred_element_type=jnp.float32)
            acc[q, at, :] = part if first else acc[q, at, :] + part
            if send:
                x_copy(q, i).start()

        each(low, high, product)

    whole = slice(None)

    def out_at(q):
        return slice((q - 2) * qw, (q - 1) * qw)

    def finish(q, at_depth):
        def product(i):
            at = tile_at(i)
            x_copy(q - 2, i).wait_recv()
            part = jnp.dot(
                hid[at, at_depth], wbuf[q, at_depth, :], preferred_element_type=jnp.float32)
            kv_ref[at, out_at(q)] = (acc[q, at, :] + precv[q - 2, at, :] + part).astype(jnp.bfloat16)

        each(0, tiles, product)

    def spread(i):
        h_recv(i, t).wait_recv()
        h_spread(0, i).start()
        h_spread(1, i).start()

    def partial(i):
        h_recv(i, across).wait_recv()
        h_spread(2, i).start()
        h_recv(i, mate).wait_recv()
        h_recv(i, cross).wait_recv()
        at = tile_at(i)
        racc[0, at, :] = jnp.dot(hbuf[at, :], wbuf[0, far, :], preferred_element_type=jnp.float32)
        q_copy(i).start()

    def give_back(i):
        at = tile_at(i)
        part = jnp.dot(hbuf[at, :], wbuf[2, far, :], preferred_element_type=jnp.float32)
        q_copy(i).wait_recv()
        racc[1, at, :] = part + rx[at, :]
        b_copy(i).start()

    weigh()

    @pl.when(outer)
    def _():
        mid, away, end = f + inward, f + 2 * inward, f + 3 * inward
        send_own(1, inward)
        send_own(2, inward)
        hid_copy.wait()
        for i in range(tiles - 1):
            h_copy(i).start()
        send_own(3, inward)
        h_copy(tiles - 1).start()
        gather_tokens()
        take(0, mid)
        add(0, near, first=True, send=True)
        score()
        take(1, mid)
        add(1, near, first=True)
        take(2, mid)
        add(2, near, first=True)
        take(3, mid)
        add(3, near, first=True)
        reward()
        take(1, away)
        take(1, end)
        add(1, far, send=True)
        advantage()

        def returned(i):
            at = tile_at(i)
            x_copy(0, i).wait_recv()
            b_copy(i).wait_recv()
            kv_ref[at, out_at(2)] = (acc[2, at, :] + precv[0, at, :] + rret[at, :]).astype(jnp.bfloat16)

        each(0, tiles - 2, returned)
        take(3, away)
        add(3, block_at(away))
        each(tiles - 2, tiles - 1, returned)
        take(3, end)
        finish(3, block_at(end))
        each(tiles - 1, tiles, returned)

    @pl.when(inner)
    def _():
        edge, away, end = f + outward, f + inward, f + 2 * inward
        for q in range(1, 4):
            send_own(q, outward)
        take(0, edge, inward)
        send_own(1, inward)
        hid_copy.wait()
        gather_tokens()
        take(1, edge, inward)
        send_own(2, inward)
        take(0, away)
        take(0, end)
        score()
        add(0, whole, first=True, send=True)
        take(2, edge, inward)
        send_own(3, inward)
        take(1, away, outward)
        take(1, end, outward)
        reward()
        spread(0)
        add(1, whole, first=True, send=True, high=tiles // 2)
        partial(0)
        spread(1)
        take(2, away)
        partial(1)
        add(1, whole, first=True, send=True, low=tiles // 2)
        spread(2)
        take(2, end)
        give_back(0)
        give_back(1)
        partial(2)
        add(2, near, first=True)
        take(3, edge, inward)
        take(3, away, outward)
        give_back(2)
        spread(3)
        take(3, end, outward)
        add(3, near, first=True)
        partial(3)
        finish(2, far)
        give_back(3)
        advantage()
        finish(3, far)

    for q in range(2):
        each(0, tiles, lambda i: x_copy(q, i).wait_send())
    r_copy().wait_send()
    for k in range(1, n):
        v_copy(k, f).wait_send()
    each(1, plane, lambda k: s_copy(k, me).wait_send())
    each(1, n, lambda k: z_copy(k, f).wait_send())
    for r in range(parts):
        for q in range(4):
            w_copy(q, f, r, inward).wait_send()

    @pl.when(outer)
    def _():
        each(0, tiles, lambda i: h_copy(i).wait_send())

    @pl.when(inner)
    def _():
        for r in range(parts):
            for q in range(4):
                w_copy(q, f, r, outward).wait_send()
                w_copy(q, f + outward, r, inward).wait_send()
                if q % 2:
                    w_copy(q, f + inward, r, outward).wait_send()
                    w_copy(q, f + 2 * inward, r, outward).wait_send()

        def sent(i):
            for k in range(3):
                h_spread(k, i).wait_send()
            q_copy(i).wait_send()
            b_copy(i).wait_send()

        each(0, tiles, sent)


def solution(mesh):
    n, nt, ns = mesh.shape["fsdp"], mesh.shape["tp"], mesh.shape["sect"]

    def local(hidden, kv_weight, readout, lengths, prompt_mask, group_ids):
        tok, depth = hidden.shape
        rows, width = kv_weight.shape
        parts = max(1, min(2, rows // 256))
        cw = width // 2
        plane = nt * ns
        n_seq = lengths.shape[1]
        tile = min(256, tok)
        in_line = n == 4 and nt == 4 and ns == 2 and rows % 1024 == 0 and cw % 256 == 0 and tok % 1024 == 0
        dma = pltpu.SemaphoreType.DMA
        vmem, smem, anywhere = (
            pl.BlockSpec(memory_space=pltpu.VMEM),
            pl.BlockSpec(memory_space=pltpu.SMEM),
            pl.BlockSpec(memory_space=pl.ANY),
        )
        if in_line:
            body = functools.partial(line_kernel, nt, ns, parts, tile)
            tiles = tok // tile
            qw = cw // 2
            scratch = [
                pltpu.VMEM((tok, depth), jnp.bfloat16),
                pltpu.VMEM((4, depth, qw), jnp.bfloat16),
                pltpu.VMEM((4, tok, qw), jnp.float32),
                pltpu.VMEM((2, tok, qw), jnp.float32),
                pltpu.VMEM((tok, 2 * rows), jnp.bfloat16),
                pltpu.VMEM((2, tok, qw), jnp.float32),
                pltpu.VMEM((tok, qw), jnp.float32),
                pltpu.VMEM((tok, qw), jnp.float32),
                pltpu.VMEM((8, tok), jnp.float32),
                pltpu.VMEM((8, depth), jnp.float32),
                pltpu.VMEM((1, cw), jnp.float32),
                pltpu.VMEM((n, rows // 128, 128), jnp.float32),
                pltpu.VMEM((plane, 8, 128), jnp.float32),
                pltpu.VMEM((n, 2, 8, 128), jnp.float32),
                dma, dma((4,)),
                dma((2, 4, parts, n)), dma((4, parts, n)),
                dma((2, tiles)), dma((2, tiles)),
                dma, dma,
                dma((n,)), dma((n,)),
                dma((plane,)), dma((plane,)),
                dma((n,)), dma((n,)),
                dma((3, tiles)), dma((tiles, nt)),
                dma((tiles,)), dma((tiles,)),
                dma((tiles,)), dma((tiles,)),
            ]
        else:
            body = functools.partial(kernel, n, nt, ns, parts, tile)
            scratch = [
                pltpu.VMEM((tok, depth), jnp.bfloat16),
                pltpu.VMEM((2, depth, cw), jnp.bfloat16),
                pltpu.VMEM((2, tok, cw), jnp.float32),
                pltpu.VMEM((tok, cw), jnp.float32),
                pltpu.VMEM((8, tok), jnp.float32),
                pltpu.VMEM((plane, 8, cw), jnp.float32),
                pltpu.VMEM((n, 2, 8, 128), jnp.float32),
                dma, dma((2, parts)),
                dma((2, 2, parts, n)), dma((2, parts, n)),
                dma, dma,
                dma((plane,)), dma((plane,)),
                dma((n,)), dma((n,)),
            ]
        kv, adv = pl.pallas_call(
            body,
            out_shape=(
                pltpu.VMEM((tok, width // 2), jnp.bfloat16),
                pltpu.VMEM((1, n_seq), jnp.float32),
            ),
            in_specs=[anywhere, anywhere, vmem, vmem, smem, smem],
            out_specs=(vmem, vmem),
            scratch_shapes=scratch,
            compiler_params=pltpu.CompilerParams(collective_id=0, has_side_effects=True),
        )(hidden, kv_weight, readout[None, :], prompt_mask[None, :], lengths, group_ids)
        return kv, adv[0]

    return jax.shard_map(
        local,
        mesh=mesh,
        in_specs=(
            P("fsdp", "sect"),
            P(("sect", "fsdp"), "tp"),
            P(("tp", "sect")),
            P("fsdp", None),
            P("fsdp"),
            P("fsdp"),
        ),
        out_specs=(P("fsdp", ("tp", "sect")), P("fsdp")),
        check_vma=False,
    )
```

```python
import functools

import jax
import jax.numpy as jnp
from jax import lax
from jax.experimental import pallas as pl
from jax.experimental.pallas import tpu as pltpu
from jax.sharding import PartitionSpec as P

MESH = pl.DeviceIdType.MESH


def kernel(
    n, nt, ns, parts, tile,
    hid_any, w_any, ro_ref, mask_ref, len_ref, gid_ref,
    kv_ref, adv_ref,
    hid, wbuf, acc, precv, member, sbuf, zbuf,
    hid_sem, own_sem, wsend, wrecv, xsend, xrecv, ssend, srecv, zsend, zrecv,
):
    f, t, s = lax.axis_index("fsdp"), lax.axis_index("tp"), lax.axis_index("sect")
    plane = nt * ns
    me = t * ns + s
    rows, width = w_any.shape
    cw = width // 2
    piece = rows // parts
    by_piece = piece % 128 == 0
    tok = hid.shape[0]

    def plane_id(k):
        other = lax.rem(me + k, plane)
        return {"tp": lax.div(other, ns), "sect": lax.rem(other, ns)}

    def line_id(k):
        return {"fsdp": lax.rem(f + k, n)}

    def cols(c):
        side = s if c else 1 - s
        return pl.ds(pl.multiple_of(side * cw, cw), cw)

    def depth_at(j, r):
        return pl.ds(pl.multiple_of(j * rows + r * piece, piece), piece)

    def own_rows(c, r):
        return w_any.at[r * piece:(r + 1) * piece, cols(c)]

    def w_copy(c, j, r, step, own):
        place = wbuf.at[c, depth_at(j, r), :]
        return pltpu.make_async_remote_copy(
            src_ref=own_rows(c, r) if own else place,
            dst_ref=place,
            send_sem=wsend.at[0 if step > 0 else 1, c, r, j],
            recv_sem=wrecv.at[c, r, j],
            device_id={"fsdp": f + step},
            device_id_type=MESH,
        )

    def x_copy():
        return pltpu.make_async_remote_copy(
            src_ref=acc.at[0],
            dst_ref=precv,
            send_sem=xsend,
            recv_sem=xrecv,
            device_id={"sect": 1 - s},
            device_id_type=MESH,
        )

    def s_copy(k, slot):
        return pltpu.make_async_remote_copy(
            src_ref=sbuf.at[slot],
            dst_ref=sbuf.at[slot],
            send_sem=ssend.at[k],
            recv_sem=srecv.at[slot],
            device_id=plane_id(k),
            device_id_type=MESH,
        )

    def z_copy(k, slot):
        return pltpu.make_async_remote_copy(
            src_ref=zbuf.at[slot],
            dst_ref=zbuf.at[slot],
            send_sem=zsend.at[k],
            recv_sem=zrecv.at[slot],
            device_id=line_id(k),
            device_id_type=MESH,
        )

    def each(low, high, body):
        def step(i, carry):
            body(i)
            return carry

        lax.fori_loop(low, high, step, 0)

    barrier = pltpu.get_barrier_semaphore()
    each(1, n, lambda k: pl.semaphore_signal(
        barrier, inc=1, device_id=line_id(k), device_id_type=MESH))
    each(1, plane, lambda k: pl.semaphore_signal(
        barrier, inc=1, device_id=plane_id(k), device_id_type=MESH))

    def own_copy(c, r):
        return pltpu.make_async_copy(
            own_rows(c, r), wbuf.at[c, depth_at(f, r), :], own_sem.at[c, r])

    def send_own(c, step):
        for r in range(parts):
            w_copy(c, f, r, step, True).start()

    pl.semaphore_wait(barrier, n - 1 + plane - 1)

    @pl.when(f < n - 1)
    def _():
        send_own(0, 1)

    @pl.when(f > 0)
    def _():
        send_own(0, -1)

    @pl.when(f == 0)
    def _():
        send_own(1, 1)

    @pl.when(f == n - 1)
    def _():
        send_own(1, -1)

    hid_copy = pltpu.make_async_copy(hid_any, hid, hid_sem)
    for c in range(2):
        for r in range(parts):
            own_copy(c, r).start()
    hid_copy.start()

    place = lax.broadcasted_iota(jnp.int32, (8, tok), 1)
    seq = lax.broadcasted_iota(jnp.int32, (8, tok), 0)
    inside = jnp.zeros((8, tok), jnp.bool_)
    start = jnp.int32(0)
    n_seq = len_ref.shape[1]
    for j in range(n_seq):
        finish = start + len_ref[0, j]
        inside = inside | ((seq == j) & (place >= start) & (place < finish))
        start = finish
    member[...] = inside.astype(jnp.float32) * mask_ref[...].astype(jnp.float32)

    def add(c, depth, first):
        def product(i, carry):
            at = pl.ds(pl.multiple_of(i * tile, tile), tile)
            part = jnp.dot(
                hid[at, depth], wbuf[c, depth, :], preferred_element_type=jnp.float32)
            acc[c, at, :] = part if first else acc[c, at, :] + part
            return carry

        lax.fori_loop(0, tok // tile, product, 0)

    def arrive(c, j, r, step):
        w_copy(c, j, r, -step, False).wait_recv()

        @pl.when((f + step >= 0) & (f + step < n))
        def _():
            w_copy(c, j, r, step, False).start()

        if by_piece:
            add(c, depth_at(j, r), False)

    for c in range(2):
        for r in range(parts):
            own_copy(c, r).wait()
        if c == 0:
            hid_copy.wait()
        if by_piece:
            add(c, pl.ds(pl.multiple_of(f * rows, rows), rows), True)

        def visit(d, c=c):
            left, right = f - d, f + d
            for r in range(parts):
                @pl.when(left >= 0)
                def _():
                    arrive(c, left, r, 1)

                @pl.when(right < n)
                def _():
                    arrive(c, right, r, -1)

            if c == 0:
                @pl.when((d == f) & (f < n - 1))
                def _():
                    send_own(1, 1)

                @pl.when((d == n - 1 - f) & (f > 0))
                def _():
                    send_own(1, -1)

        each(1, n, visit)
        if not by_piece:
            add(c, slice(None), True)
        if c == 0:
            x_copy().start()

    x_copy().wait_recv()

    def finish_rows(i, carry):
        at = pl.ds(pl.multiple_of(i * tile, tile), tile)
        projected = acc[1, at, :] + precv[at, :]
        kv_ref[at, :] = projected.astype(jnp.bfloat16)
        chosen = member[:, at].astype(jnp.bfloat16)
        rest = projected
        for _ in range(3):
            digits = rest.astype(jnp.bfloat16)
            carry += jnp.dot(chosen, digits, preferred_element_type=jnp.float32)
            rest = rest - digits.astype(jnp.float32)
        return carry

    total = lax.fori_loop(
        0, tok // tile, finish_rows, jnp.zeros((8, cw), jnp.float32)) * ro_ref[...]
    sbuf[me] = total
    each(1, plane, lambda k: s_copy(k, me).start())
    count = jnp.sum(member[...], axis=1, keepdims=True)
    each(1, plane, lambda k: s_copy(k, lax.rem(me + k, plane)).wait_recv())
    seq_sum = jnp.sum(jnp.sum(sbuf[...], axis=0), axis=1, keepdims=True)
    reward = seq_sum / jnp.sqrt(jnp.maximum(count, 1.0))

    row = lax.broadcasted_iota(jnp.int32, (8, 128), 0)
    lane = lax.broadcasted_iota(jnp.int32, (8, 128), 1)
    row_gid = jnp.full((8, 128), -1, jnp.int32)
    lane_gid = jnp.full((8, 128), -2, jnp.int32)
    for j in range(n_seq):
        row_gid = jnp.where(row == j, gid_ref[j], row_gid)
        lane_gid = jnp.where(lane == j, gid_ref[j], lane_gid)
    reward = jnp.broadcast_to(reward, (8, 128))
    zbuf[f, 0] = reward
    zbuf[f, 1] = row_gid.astype(jnp.float32)
    each(1, n, lambda k: z_copy(k, f).start())
    mine = jnp.sum(jnp.where(row == lane, reward, 0.0), axis=0, keepdims=True)
    each(1, n, lambda k: z_copy(k, lax.rem(f + k, n)).wait_recv())
    same = (zbuf[:, 1] == lane_gid.astype(jnp.float32)[None]).astype(jnp.float32)
    rewards = zbuf[:, 0]

    def over(value):
        return jnp.sum(jnp.sum(value, axis=0), axis=0, keepdims=True)

    size = jnp.maximum(over(same), 1.0)
    mean = over(same * rewards) / size
    var = over(same * (rewards - mean[None]) ** 2) / size
    adv_ref[...] = ((mine - mean) / jnp.sqrt(var + 1.0))[:, :n_seq]

    each(1, plane, lambda k: s_copy(k, me).wait_send())
    each(1, n, lambda k: z_copy(k, f).wait_send())
    x_copy().wait_send()
    for c in range(2):
        def sent(j, c=c):
            for r in range(parts):
                @pl.when((j <= f) & (f < n - 1))
                def _():
                    w_copy(c, j, r, 1, False).wait_send()

                @pl.when((j >= f) & (f > 0))
                def _():
                    w_copy(c, j, r, -1, False).wait_send()

        each(0, n, sent)


def line_kernel(
    nt, ns, parts, tile, blocks,
    hid_any, w_any, ro_ref, mask_ref, len_ref, gid_ref,
    kv_ref, adv_ref,
    hid, wbuf, acc, precv, hbuf, racc, rx, rret, member, gsum, robuf, vbuf, sbuf, zbuf,
    hid_sem, own_sem, wsend, wrecv, xsend, xrecv, rsend, rrecv,
    vsend, vrecv, ssend, srecv, zsend, zrecv,
    hsend, hrecv, qsend, qrecv, bsend, brecv,
):
    n = 4
    f, t, s = lax.axis_index("fsdp"), lax.axis_index("tp"), lax.axis_index("sect")
    plane = nt * ns
    me = t * ns + s
    rows, width = w_any.shape
    cw = width // 2
    qw = cw // 2
    piece = rows // parts
    tok, depth = hid.shape
    tiles = tok // tile
    blk = tok // blocks
    share = blk // nt
    inward = jnp.where(f < 2, 1, -1)
    outward = -inward
    outer = (f == 0) | (f == n - 1)
    inner = (f == 1) | (f == n - 2)
    near_at = jnp.where(f < 2, 0, 2 * rows)
    near = pl.ds(pl.multiple_of(near_at, rows), 2 * rows)
    far = pl.ds(pl.multiple_of(2 * rows - near_at, rows), 2 * rows)
    mate = lax.div(t, 2) * 2 + (1 - lax.rem(t, 2))
    across = lax.rem(t + 2, 4)
    cross = lax.rem(mate + 2, 4)

    def plane_id(k):
        other = lax.rem(me + k, plane)
        return {"tp": lax.div(other, ns), "sect": lax.rem(other, ns)}

    def line_id(k):
        return {"fsdp": lax.rem(f + k, n)}

    def cols(q):
        side = s if q >= 2 else 1 - s
        return pl.ds(pl.multiple_of(side * cw + (q % 2) * qw, qw), qw)

    def depth_at(j, r):
        return pl.ds(pl.multiple_of(j * rows + r * piece, piece), piece)

    def block_at(j):
        return pl.ds(pl.multiple_of(j * rows, rows), rows)

    def tile_at(i):
        return pl.ds(pl.multiple_of(i * tile, tile), tile)

    def blk_at(i):
        return pl.ds(pl.multiple_of(i * blk, blk), blk)

    def share_at(i, p):
        return pl.ds(pl.multiple_of(i * blk + p * share, share), share)

    def remote(src, dst, send, recv, device):
        return pltpu.make_async_remote_copy(
            src_ref=src, dst_ref=dst, send_sem=send, recv_sem=recv,
            device_id=device, device_id_type=MESH)

    def w_copy(q, j, r, step, own=False):
        place = wbuf.at[q, depth_at(j, r), :]
        src = w_any.at[r * piece:(r + 1) * piece, cols(q)] if own else place
        toward = 0 if step is inward else 1
        return remote(src, place, wsend.at[toward, q, r, j], wrecv.at[q, r, j], {"fsdp": f + step})

    def x_copy(q, i):
        at = tile_at(i)
        return remote(acc.at[q, at], precv.at[q, at], xsend.at[q, i], xrecv.at[q, i], {"sect": 1 - s})

    def h_copy(i):
        at = share_at(i, t)
        return remote(hid.at[at, far], hbuf.at[at], hsend.at[0, i], hrecv.at[i, t], {"fsdp": f + inward})

    def h_spread(k, i):
        p = (t, t, across)[k]
        to = (mate, across, mate)[k]
        at = share_at(i, p)
        return remote(hbuf.at[at], hbuf.at[at], hsend.at[k, i], hrecv.at[i, p], {"tp": to})

    def h_recv(i, p):
        at = share_at(i, p)
        return remote(hbuf.at[at], hbuf.at[at], hsend.at[0, i], hrecv.at[i, p], {"tp": mate})

    def q_copy(i):
        at = blk_at(i)
        return remote(racc.at[0, at], rx.at[at], qsend.at[i], qrecv.at[i], {"sect": 1 - s})

    def b_copy(i):
        at = blk_at(i)
        return remote(racc.at[1, at], rret.at[at], bsend.at[i], brecv.at[i], {"fsdp": f + outward})

    def r_copy():
        return remote(ro_ref, robuf, rsend, rrecv, {"sect": 1 - s})

    def v_copy(k, slot):
        return remote(vbuf.at[slot], vbuf.at[slot], vsend.at[k], vrecv.at[slot], line_id(k))

    def s_copy(k, slot):
        return remote(sbuf.at[slot], sbuf.at[slot], ssend.at[k], srecv.at[slot], plane_id(k))

    def z_copy(k, slot):
        return remote(zbuf.at[slot], zbuf.at[slot], zsend.at[k], zrecv.at[slot], line_id(k))

    def own_copy(q):
        return pltpu.make_async_copy(
            w_any.at[:, cols(q)], wbuf.at[q, block_at(f), :], own_sem.at[q])

    def each(low, high, body):
        def step(i, carry):
            body(i)
            return carry

        lax.fori_loop(low, high, step, 0)

    def send_own(q, step):
        for r in range(parts):
            w_copy(q, f, r, step, own=True).start()

    def take(q, j, step=None, low=0, high=parts):
        for r in range(low, high):
            w_copy(q, j, r, outward).wait_recv()
            if step is not None:
                w_copy(q, j, r, step).start()

    barrier = pltpu.get_barrier_semaphore()
    each(1, n, lambda k: pl.semaphore_signal(
        barrier, inc=1, device_id=line_id(k), device_id_type=MESH))
    each(1, plane, lambda k: pl.semaphore_signal(
        barrier, inc=1, device_id=plane_id(k), device_id_type=MESH))
    for q in (2, 3, 0, 1):
        own_copy(q).start()
    hid_copy = pltpu.make_async_copy(hid_any, hid, hid_sem)
    hid_copy.start()
    pl.semaphore_wait(barrier, n - 1 + plane - 1)

    send_own(0, inward)

    @pl.when(inner)
    def _():
        send_own(0, outward)

    r_copy().start()

    place = lax.broadcasted_iota(jnp.int32, (8, tok), 1)
    seq = lax.broadcasted_iota(jnp.int32, (8, tok), 0)
    inside = jnp.zeros((8, tok), jnp.bool_)
    start = jnp.int32(0)
    n_seq = len_ref.shape[1]
    for j in range(n_seq):
        finish = start + len_ref[0, j]
        inside = inside | ((seq == j) & (place >= start) & (place < finish))
        start = finish
    member[...] = inside.astype(jnp.float32) * mask_ref[...].astype(jnp.float32)

    def weigh():
        line = lax.broadcasted_iota(jnp.int32, (8, qw), 0)
        total = jnp.zeros((8, rows), jnp.float32)
        for q in (2, 3, 0, 1):
            if q == 0:
                r_copy().wait_recv()
            own_copy(q).wait()
            values = (ro_ref if q >= 2 else robuf)[:, (q % 2) * qw:(q % 2 + 1) * qw]
            rest = jnp.broadcast_to(values, (8, qw))
            digits = jnp.zeros((8, qw), jnp.float32)
            for k in range(3):
                digit = rest.astype(jnp.bfloat16).astype(jnp.float32)
                digits = jnp.where(line == k, digit, digits)
                rest = rest - digit
            total += lax.dot_general(
                digits.astype(jnp.bfloat16), wbuf[q, block_at(f), :],
                (((1,), (1,)), ((), ())), preferred_element_type=jnp.float32)
        total = jnp.sum(total, axis=0, keepdims=True)
        for i in range(rows // 128):
            vbuf[f, i:i + 1, :] = total[:, i * 128:(i + 1) * 128]
        for k in range(1, n):
            v_copy(k, f).start()

    def gather_tokens():
        chosen = member[...].astype(jnp.bfloat16)
        step = 512 if depth % 512 == 0 else 128

        def part(i):
            at = pl.ds(pl.multiple_of(i * step, step), step)
            gsum[:, at] = jnp.dot(chosen, hid[:, at], preferred_element_type=jnp.float32)

        each(0, depth // step, part)

    def score():
        for k in range(1, n):
            v_copy(k, lax.rem(f + k, n)).wait_recv()
        total = jnp.zeros((8, 128), jnp.float32)
        for j in range(n):
            for i in range(rows // 128):
                at = j * rows + i * 128
                total += gsum[:, at:at + 128] * vbuf[j, i:i + 1, :]
        sbuf[me] = jnp.broadcast_to(jnp.sum(total, axis=1, keepdims=True), (8, 128))
        each(1, plane, lambda k: s_copy(k, me).start())

    row = lax.broadcasted_iota(jnp.int32, (8, 128), 0)
    lane = lax.broadcasted_iota(jnp.int32, (8, 128), 1)

    def reward():
        count = jnp.sum(member[...], axis=1, keepdims=True)
        each(1, plane, lambda k: s_copy(k, lax.rem(me + k, plane)).wait_recv())
        seq_sum = jnp.sum(sbuf[...], axis=0)
        row_gid = jnp.full((8, 128), -1, jnp.int32)
        for j in range(n_seq):
            row_gid = jnp.where(row == j, gid_ref[j], row_gid)
        zbuf[f, 0] = seq_sum / jnp.sqrt(jnp.maximum(count, 1.0))
        zbuf[f, 1] = row_gid.astype(jnp.float32)
        each(1, n, lambda k: z_copy(k, f).start())

    def advantage():
        each(1, n, lambda k: z_copy(k, lax.rem(f + k, n)).wait_recv())
        lane_gid = jnp.full((8, 128), -2, jnp.int32)
        for j in range(n_seq):
            lane_gid = jnp.where(lane == j, gid_ref[j], lane_gid)
        mine = jnp.sum(jnp.where(row == lane, zbuf[f, 0], 0.0), axis=0, keepdims=True)
        same = (zbuf[:, 1] == lane_gid.astype(jnp.float32)[None]).astype(jnp.float32)
        rewards = zbuf[:, 0]

        def over(value):
            return jnp.sum(jnp.sum(value, axis=0), axis=0, keepdims=True)

        size = jnp.maximum(over(same), 1.0)
        mean = over(same * rewards) / size
        var = over(same * (rewards - mean[None]) ** 2) / size
        adv_ref[...] = ((mine - mean) / jnp.sqrt(var + 1.0))[:, :n_seq]

    def add(q, at_depth, first=False, send=False, low=0, high=tiles):
        def product(i):
            at = tile_at(i)
            part = jnp.dot(
                hid[at, at_depth], wbuf[q, at_depth, :], preferred_element_type=jnp.float32)
            acc[q, at, :] = part if first else acc[q, at, :] + part
            if send:
                x_copy(q, i).start()

        each(low, high, product)

    whole = slice(None)

    def out_at(q):
        return slice((q - 2) * qw, (q - 1) * qw)

    def finish(q, at_depth):
        def product(i):
            at = tile_at(i)
            x_copy(q - 2, i).wait_recv()
            part = jnp.dot(
                hid[at, at_depth], wbuf[q, at_depth, :], preferred_element_type=jnp.float32)
            kv_ref[at, out_at(q)] = (acc[q, at, :] + precv[q - 2, at, :] + part).astype(jnp.bfloat16)

        each(0, tiles, product)

    def spread(i):
        h_recv(i, t).wait_recv()
        h_spread(0, i).start()
        h_spread(1, i).start()

    def relay(i):
        h_recv(i, across).wait_recv()
        h_spread(2, i).start()

    def partial(i):
        h_recv(i, mate).wait_recv()
        h_recv(i, cross).wait_recv()
        at = blk_at(i)
        racc[0, at, :] = jnp.dot(hbuf[at, :], wbuf[0, far, :], preferred_element_type=jnp.float32)
        q_copy(i).start()

    def give_back(i):
        at = blk_at(i)
        part = jnp.dot(hbuf[at, :], wbuf[2, far, :], preferred_element_type=jnp.float32)
        q_copy(i).wait_recv()
        racc[1, at, :] = part + rx[at, :]
        b_copy(i).start()

    def returned(i):
        at = blk_at(i)
        b_copy(i).wait_recv()
        kv_ref[at, out_at(2)] = (acc[2, at, :] + precv[0, at, :] + rret[at, :]).astype(jnp.bfloat16)

    weigh()

    @pl.when(outer)
    def _():
        mid, away, end = f + inward, f + 2 * inward, f + 3 * inward
        send_own(1, inward)
        send_own(2, inward)
        hid_copy.wait()
        each(0, 5, lambda i: h_copy(i).start())
        for r in range(parts):
            w_copy(3, f, r, inward, own=True).start()
            h_copy(5 + r).start()
        each(5 + parts, blocks, lambda i: h_copy(i).start())
        gather_tokens()
        take(0, mid)
        add(0, near, first=True, send=True)
        score()
        for q in range(1, 4):
            take(q, mid)
            add(q, near, first=True)
        reward()
        take(1, away)
        take(1, end)
        add(1, far, send=True)
        take(3, away)
        add(3, block_at(away))
        each(0, tiles, lambda i: x_copy(0, i).wait_recv())
        each(0, 6, returned)
        advantage()
        take(3, end, high=parts - 1)
        for r in range(parts - 1):
            add(3, depth_at(end, r))
        take(3, end, low=parts - 1)
        finish(3, depth_at(end, parts - 1))
        each(6, blocks, returned)

    @pl.when(inner)
    def _():
        edge, away, end = f + outward, f + inward, f + 2 * inward
        for q in range(1, 4):
            send_own(q, outward)
        take(0, edge, inward)
        send_own(1, inward)
        hid_copy.wait()
        gather_tokens()
        take(1, edge, inward)
        send_own(3, inward)
        take(0, away)
        take(0, end)
        score()
        add(0, whole, first=True, send=True)
        take(2, edge, inward)
        send_own(2, inward)
        take(1, away, outward)
        add(1, near, first=True)
        spread(0)
        spread(1)
        take(1, end, outward)
        relay(0)
        reward()
        add(1, far, send=True, high=tiles // 2)
        spread(2)
        partial(0)
        relay(1)
        spread(3)
        partial(1)
        take(3, away, outward)
        add(1, far, send=True, low=tiles // 2)
        relay(2)
        spread(4)
        partial(2)
        relay(3)
        partial(3)
        take(3, edge, inward, high=1)
        add(2, near, first=True)
        relay(4)
        spread(5)
        partial(4)
        take(2, end)
        take(2, away)
        take(3, edge, inward, low=1)
        each(0, 5, give_back)
        relay(5)
        spread(6)
        partial(5)
        finish(2, far)
        spread(7)
        give_back(5)
        relay(6)
        add(3, near, first=True)
        take(3, end, outward)
        partial(6)
        relay(7)
        partial(7)
        give_back(6)
        finish(3, far)
        give_back(7)
        advantage()

    for q in range(2):
        each(0, tiles, lambda i: x_copy(q, i).wait_send())
    r_copy().wait_send()
    for k in range(1, n):
        v_copy(k, f).wait_send()
    each(1, plane, lambda k: s_copy(k, me).wait_send())
    each(1, n, lambda k: z_copy(k, f).wait_send())
    for r in range(parts):
        for q in range(4):
            w_copy(q, f, r, inward).wait_send()

    @pl.when(outer)
    def _():
        each(0, blocks, lambda i: h_copy(i).wait_send())

    @pl.when(inner)
    def _():
        for r in range(parts):
            for q in range(4):
                w_copy(q, f, r, outward).wait_send()
                w_copy(q, f + outward, r, inward).wait_send()
                if q % 2:
                    w_copy(q, f + inward, r, outward).wait_send()
                    w_copy(q, f + 2 * inward, r, outward).wait_send()

        def sent(i):
            for k in range(3):
                h_spread(k, i).wait_send()
            q_copy(i).wait_send()
            b_copy(i).wait_send()

        each(0, blocks, sent)


def solution(mesh):
    n, nt, ns = mesh.shape["fsdp"], mesh.shape["tp"], mesh.shape["sect"]

    def local(hidden, kv_weight, readout, lengths, prompt_mask, group_ids):
        tok, depth = hidden.shape
        rows, width = kv_weight.shape
        parts = max(1, min(2, rows // 256))
        cw = width // 2
        plane = nt * ns
        n_seq = lengths.shape[1]
        tile = min(256, tok)
        in_line = n == 4 and nt == 4 and ns == 2 and rows % 1024 == 0 and cw % 256 == 0 and tok % 1024 == 0
        dma = pltpu.SemaphoreType.DMA
        vmem, smem, anywhere = (
            pl.BlockSpec(memory_space=pltpu.VMEM),
            pl.BlockSpec(memory_space=pltpu.SMEM),
            pl.BlockSpec(memory_space=pl.ANY),
        )
        if in_line:
            blocks = 8
            body = functools.partial(line_kernel, nt, ns, parts, tile, blocks)
            tiles = tok // tile
            qw = cw // 2
            scratch = [
                pltpu.VMEM((tok, depth), jnp.bfloat16),
                pltpu.VMEM((4, depth, qw), jnp.bfloat16),
                pltpu.VMEM((4, tok, qw), jnp.float32),
                pltpu.VMEM((2, tok, qw), jnp.float32),
                pltpu.VMEM((tok, 2 * rows), jnp.bfloat16),
                pltpu.VMEM((2, tok, qw), jnp.float32),
                pltpu.VMEM((tok, qw), jnp.float32),
                pltpu.VMEM((tok, qw), jnp.float32),
                pltpu.VMEM((8, tok), jnp.float32),
                pltpu.VMEM((8, depth), jnp.float32),
                pltpu.VMEM((1, cw), jnp.float32),
                pltpu.VMEM((n, rows // 128, 128), jnp.float32),
                pltpu.VMEM((plane, 8, 128), jnp.float32),
                pltpu.VMEM((n, 2, 8, 128), jnp.float32),
                dma, dma((4,)),
                dma((2, 4, parts, n)), dma((4, parts, n)),
                dma((2, tiles)), dma((2, tiles)),
                dma, dma,
                dma((n,)), dma((n,)),
                dma((plane,)), dma((plane,)),
                dma((n,)), dma((n,)),
                dma((3, blocks)), dma((blocks, nt)),
                dma((blocks,)), dma((blocks,)),
                dma((blocks,)), dma((blocks,)),
            ]
        else:
            body = functools.partial(kernel, n, nt, ns, parts, tile)
            scratch = [
                pltpu.VMEM((tok, depth), jnp.bfloat16),
                pltpu.VMEM((2, depth, cw), jnp.bfloat16),
                pltpu.VMEM((2, tok, cw), jnp.float32),
                pltpu.VMEM((tok, cw), jnp.float32),
                pltpu.VMEM((8, tok), jnp.float32),
                pltpu.VMEM((plane, 8, cw), jnp.float32),
                pltpu.VMEM((n, 2, 8, 128), jnp.float32),
                dma, dma((2, parts)),
                dma((2, 2, parts, n)), dma((2, parts, n)),
                dma, dma,
                dma((plane,)), dma((plane,)),
                dma((n,)), dma((n,)),
            ]
        kv, adv = pl.pallas_call(
            body,
            out_shape=(
                pltpu.VMEM((tok, width // 2), jnp.bfloat16),
                pltpu.VMEM((1, n_seq), jnp.float32),
            ),
            in_specs=[anywhere, anywhere, vmem, vmem, smem, smem],
            out_specs=(vmem, vmem),
            scratch_shapes=scratch,
            compiler_params=pltpu.CompilerParams(collective_id=0, has_side_effects=True),
        )(hidden, kv_weight, readout[None, :], prompt_mask[None, :], lengths, group_ids)
        return kv, adv[0]

    return jax.shard_map(
        local,
        mesh=mesh,
        in_specs=(
            P("fsdp", "sect"),
            P(("sect", "fsdp"), "tp"),
            P(("tp", "sect")),
            P("fsdp", None),
            P("fsdp"),
            P("fsdp"),
        ),
        out_specs=(P("fsdp", ("tp", "sect")), P("fsdp")),
        check_vma=False,
    )
```

```python
import functools

import jax
import jax.numpy as jnp
from jax import lax
from jax.experimental import pallas as pl
from jax.experimental.pallas import tpu as pltpu
from jax.sharding import PartitionSpec as P

MESH = pl.DeviceIdType.MESH


def kernel(
    n, nt, ns, parts, tile,
    hid_any, w_any, ro_ref, mask_ref, len_ref, gid_ref,
    kv_ref, adv_ref,
    hid, wbuf, acc, precv, member, sbuf, zbuf,
    hid_sem, own_sem, wsend, wrecv, xsend, xrecv, ssend, srecv, zsend, zrecv,
):
    f, t, s = lax.axis_index("fsdp"), lax.axis_index("tp"), lax.axis_index("sect")
    plane = nt * ns
    me = t * ns + s
    rows, width = w_any.shape
    cw = width // 2
    piece = rows // parts
    by_piece = piece % 128 == 0
    tok = hid.shape[0]

    def plane_id(k):
        other = lax.rem(me + k, plane)
        return {"tp": lax.div(other, ns), "sect": lax.rem(other, ns)}

    def line_id(k):
        return {"fsdp": lax.rem(f + k, n)}

    def cols(c):
        side = s if c else 1 - s
        return pl.ds(pl.multiple_of(side * cw, cw), cw)

    def depth_at(j, r):
        return pl.ds(pl.multiple_of(j * rows + r * piece, piece), piece)

    def own_rows(c, r):
        return w_any.at[r * piece:(r + 1) * piece, cols(c)]

    def w_copy(c, j, r, step, own):
        place = wbuf.at[c, depth_at(j, r), :]
        return pltpu.make_async_remote_copy(
            src_ref=own_rows(c, r) if own else place,
            dst_ref=place,
            send_sem=wsend.at[0 if step > 0 else 1, c, r, j],
            recv_sem=wrecv.at[c, r, j],
            device_id={"fsdp": f + step},
            device_id_type=MESH,
        )

    def x_copy():
        return pltpu.make_async_remote_copy(
            src_ref=acc.at[0],
            dst_ref=precv,
            send_sem=xsend,
            recv_sem=xrecv,
            device_id={"sect": 1 - s},
            device_id_type=MESH,
        )

    def s_copy(k, slot):
        return pltpu.make_async_remote_copy(
            src_ref=sbuf.at[slot],
            dst_ref=sbuf.at[slot],
            send_sem=ssend.at[k],
            recv_sem=srecv.at[slot],
            device_id=plane_id(k),
            device_id_type=MESH,
        )

    def z_copy(k, slot):
        return pltpu.make_async_remote_copy(
            src_ref=zbuf.at[slot],
            dst_ref=zbuf.at[slot],
            send_sem=zsend.at[k],
            recv_sem=zrecv.at[slot],
            device_id=line_id(k),
            device_id_type=MESH,
        )

    def each(low, high, body):
        def step(i, carry):
            body(i)
            return carry

        lax.fori_loop(low, high, step, 0)

    barrier = pltpu.get_barrier_semaphore()
    each(1, n, lambda k: pl.semaphore_signal(
        barrier, inc=1, device_id=line_id(k), device_id_type=MESH))
    each(1, plane, lambda k: pl.semaphore_signal(
        barrier, inc=1, device_id=plane_id(k), device_id_type=MESH))

    def own_copy(c, r):
        return pltpu.make_async_copy(
            own_rows(c, r), wbuf.at[c, depth_at(f, r), :], own_sem.at[c, r])

    def send_own(c, step):
        for r in range(parts):
            w_copy(c, f, r, step, True).start()

    pl.semaphore_wait(barrier, n - 1 + plane - 1)

    @pl.when(f < n - 1)
    def _():
        send_own(0, 1)

    @pl.when(f > 0)
    def _():
        send_own(0, -1)

    @pl.when(f == 0)
    def _():
        send_own(1, 1)

    @pl.when(f == n - 1)
    def _():
        send_own(1, -1)

    hid_copy = pltpu.make_async_copy(hid_any, hid, hid_sem)
    for c in range(2):
        for r in range(parts):
            own_copy(c, r).start()
    hid_copy.start()

    place = lax.broadcasted_iota(jnp.int32, (8, tok), 1)
    seq = lax.broadcasted_iota(jnp.int32, (8, tok), 0)
    inside = jnp.zeros((8, tok), jnp.bool_)
    start = jnp.int32(0)
    n_seq = len_ref.shape[1]
    for j in range(n_seq):
        finish = start + len_ref[0, j]
        inside = inside | ((seq == j) & (place >= start) & (place < finish))
        start = finish
    member[...] = inside.astype(jnp.float32) * mask_ref[...].astype(jnp.float32)

    def add(c, depth, first):
        def product(i, carry):
            at = pl.ds(pl.multiple_of(i * tile, tile), tile)
            part = jnp.dot(
                hid[at, depth], wbuf[c, depth, :], preferred_element_type=jnp.float32)
            acc[c, at, :] = part if first else acc[c, at, :] + part
            return carry

        lax.fori_loop(0, tok // tile, product, 0)

    def arrive(c, j, r, step):
        w_copy(c, j, r, -step, False).wait_recv()

        @pl.when((f + step >= 0) & (f + step < n))
        def _():
            w_copy(c, j, r, step, False).start()

        if by_piece:
            add(c, depth_at(j, r), False)

    for c in range(2):
        for r in range(parts):
            own_copy(c, r).wait()
        if c == 0:
            hid_copy.wait()
        if by_piece:
            add(c, pl.ds(pl.multiple_of(f * rows, rows), rows), True)

        def visit(d, c=c):
            left, right = f - d, f + d
            for r in range(parts):
                @pl.when(left >= 0)
                def _():
                    arrive(c, left, r, 1)

                @pl.when(right < n)
                def _():
                    arrive(c, right, r, -1)

            if c == 0:
                @pl.when((d == f) & (f < n - 1))
                def _():
                    send_own(1, 1)

                @pl.when((d == n - 1 - f) & (f > 0))
                def _():
                    send_own(1, -1)

        each(1, n, visit)
        if not by_piece:
            add(c, slice(None), True)
        if c == 0:
            x_copy().start()

    x_copy().wait_recv()

    def finish_rows(i, carry):
        at = pl.ds(pl.multiple_of(i * tile, tile), tile)
        projected = acc[1, at, :] + precv[at, :]
        kv_ref[at, :] = projected.astype(jnp.bfloat16)
        chosen = member[:, at].astype(jnp.bfloat16)
        rest = projected
        for _ in range(3):
            digits = rest.astype(jnp.bfloat16)
            carry += jnp.dot(chosen, digits, preferred_element_type=jnp.float32)
            rest = rest - digits.astype(jnp.float32)
        return carry

    total = lax.fori_loop(
        0, tok // tile, finish_rows, jnp.zeros((8, cw), jnp.float32)) * ro_ref[...]
    sbuf[me] = total
    each(1, plane, lambda k: s_copy(k, me).start())
    count = jnp.sum(member[...], axis=1, keepdims=True)
    each(1, plane, lambda k: s_copy(k, lax.rem(me + k, plane)).wait_recv())
    seq_sum = jnp.sum(jnp.sum(sbuf[...], axis=0), axis=1, keepdims=True)
    reward = seq_sum / jnp.sqrt(jnp.maximum(count, 1.0))

    row = lax.broadcasted_iota(jnp.int32, (8, 128), 0)
    lane = lax.broadcasted_iota(jnp.int32, (8, 128), 1)
    row_gid = jnp.full((8, 128), -1, jnp.int32)
    lane_gid = jnp.full((8, 128), -2, jnp.int32)
    for j in range(n_seq):
        row_gid = jnp.where(row == j, gid_ref[j], row_gid)
        lane_gid = jnp.where(lane == j, gid_ref[j], lane_gid)
    reward = jnp.broadcast_to(reward, (8, 128))
    zbuf[f, 0] = reward
    zbuf[f, 1] = row_gid.astype(jnp.float32)
    each(1, n, lambda k: z_copy(k, f).start())
    mine = jnp.sum(jnp.where(row == lane, reward, 0.0), axis=0, keepdims=True)
    each(1, n, lambda k: z_copy(k, lax.rem(f + k, n)).wait_recv())
    same = (zbuf[:, 1] == lane_gid.astype(jnp.float32)[None]).astype(jnp.float32)
    rewards = zbuf[:, 0]

    def over(value):
        return jnp.sum(jnp.sum(value, axis=0), axis=0, keepdims=True)

    size = jnp.maximum(over(same), 1.0)
    mean = over(same * rewards) / size
    var = over(same * (rewards - mean[None]) ** 2) / size
    adv_ref[...] = ((mine - mean) / jnp.sqrt(var + 1.0))[:, :n_seq]

    each(1, plane, lambda k: s_copy(k, me).wait_send())
    each(1, n, lambda k: z_copy(k, f).wait_send())
    x_copy().wait_send()
    for c in range(2):
        def sent(j, c=c):
            for r in range(parts):
                @pl.when((j <= f) & (f < n - 1))
                def _():
                    w_copy(c, j, r, 1, False).wait_send()

                @pl.when((j >= f) & (f > 0))
                def _():
                    w_copy(c, j, r, -1, False).wait_send()

        each(0, n, sent)


def line_kernel(
    nt, ns, parts, tile, blocks,
    hid_any, w_any, ro_any, mask_any, len_any, gid_any,
    kv_ref, adv_ref,
    ro_ref, mask_ref, len_ref, gid_ref, small_sem,
    hid, wbuf, acc, precv, hbuf, racc, rx, rret, member, gsum, robuf, vbuf, sbuf, zbuf,
    hid_sem, own_sem, wsend, wrecv, xsend, xrecv, rsend, rrecv,
    vsend, vrecv, ssend, srecv, zsend, zrecv,
    hsend, hrecv, qsend, qrecv, bsend, brecv,
):
    n = 4
    f, t, s = lax.axis_index("fsdp"), lax.axis_index("tp"), lax.axis_index("sect")
    plane = nt * ns
    me = t * ns + s
    rows, width = w_any.shape
    cw = width // 2
    qw = cw // 2
    piece = rows // parts
    tok, depth = hid.shape
    tiles = tok // tile
    blk = tok // blocks
    share = blk // nt
    inward = jnp.where(f < 2, 1, -1)
    outward = -inward
    outer = (f == 0) | (f == n - 1)
    inner = (f == 1) | (f == n - 2)
    near_at = jnp.where(f < 2, 0, 2 * rows)
    near = pl.ds(pl.multiple_of(near_at, rows), 2 * rows)
    far = pl.ds(pl.multiple_of(2 * rows - near_at, rows), 2 * rows)
    mate = lax.div(t, 2) * 2 + (1 - lax.rem(t, 2))
    across = lax.rem(t + 2, 4)
    cross = lax.rem(mate + 2, 4)

    def plane_id(k):
        other = lax.rem(me + k, plane)
        return {"tp": lax.div(other, ns), "sect": lax.rem(other, ns)}

    def line_id(k):
        return {"fsdp": lax.rem(f + k, n)}

    def cols(q):
        side = s if q >= 2 else 1 - s
        return pl.ds(pl.multiple_of(side * cw + (q % 2) * qw, qw), qw)

    def depth_at(j, r):
        return pl.ds(pl.multiple_of(j * rows + r * piece, piece), piece)

    def block_at(j):
        return pl.ds(pl.multiple_of(j * rows, rows), rows)

    def tile_at(i):
        return pl.ds(pl.multiple_of(i * tile, tile), tile)

    def blk_at(i):
        return pl.ds(pl.multiple_of(i * blk, blk), blk)

    def share_at(i, p):
        return pl.ds(pl.multiple_of(i * blk + p * share, share), share)

    def remote(src, dst, send, recv, device):
        return pltpu.make_async_remote_copy(
            src_ref=src, dst_ref=dst, send_sem=send, recv_sem=recv,
            device_id=device, device_id_type=MESH)

    def w_copy(q, j, r, step, own=False):
        place = wbuf.at[q, depth_at(j, r), :]
        src = w_any.at[r * piece:(r + 1) * piece, cols(q)] if own else place
        toward = 0 if step is inward else 1
        return remote(src, place, wsend.at[toward, q, r, j], wrecv.at[q, r, j], {"fsdp": f + step})

    def x_copy(q, i):
        at = tile_at(i)
        return remote(acc.at[q, at], precv.at[q, at], xsend.at[q, i], xrecv.at[q, i], {"sect": 1 - s})

    def h_copy(i):
        at = share_at(i, t)
        return remote(hid.at[at, far], hbuf.at[at], hsend.at[0, i], hrecv.at[i, t], {"fsdp": f + inward})

    def h_spread(k, i):
        p = (t, t, across)[k]
        to = (mate, across, mate)[k]
        at = share_at(i, p)
        return remote(hbuf.at[at], hbuf.at[at], hsend.at[k, i], hrecv.at[i, p], {"tp": to})

    def h_recv(i, p):
        at = share_at(i, p)
        return remote(hbuf.at[at], hbuf.at[at], hsend.at[0, i], hrecv.at[i, p], {"tp": mate})

    def q_copy(i):
        at = blk_at(i)
        return remote(racc.at[0, at], rx.at[at], qsend.at[i], qrecv.at[i], {"sect": 1 - s})

    def b_copy(i):
        at = blk_at(i)
        return remote(racc.at[1, at], rret.at[at], bsend.at[i], brecv.at[i], {"fsdp": f + outward})

    def r_copy():
        return remote(ro_ref, robuf, rsend, rrecv, {"sect": 1 - s})

    def v_copy(k, slot):
        return remote(vbuf.at[slot], vbuf.at[slot], vsend.at[k], vrecv.at[slot], line_id(k))

    def s_copy(k, slot):
        return remote(sbuf.at[slot], sbuf.at[slot], ssend.at[k], srecv.at[slot], plane_id(k))

    def z_copy(k, slot):
        return remote(zbuf.at[slot], zbuf.at[slot], zsend.at[k], zrecv.at[slot], line_id(k))

    def own_copy(q):
        return pltpu.make_async_copy(
            w_any.at[:, cols(q)], wbuf.at[q, block_at(f), :], own_sem.at[q])

    def each(low, high, body):
        def step(i, carry):
            body(i)
            return carry

        lax.fori_loop(low, high, step, 0)

    def send_own(q, step):
        for r in range(parts):
            w_copy(q, f, r, step, own=True).start()

    def take(q, j, step=None, low=0, high=parts):
        for r in range(low, high):
            w_copy(q, j, r, outward).wait_recv()
            if step is not None:
                w_copy(q, j, r, step).start()

    barrier = pltpu.get_barrier_semaphore()
    each(1, n, lambda k: pl.semaphore_signal(
        barrier, inc=1, device_id=line_id(k), device_id_type=MESH))
    each(1, plane, lambda k: pl.semaphore_signal(
        barrier, inc=1, device_id=plane_id(k), device_id_type=MESH))
    small = [
        pltpu.make_async_copy(src, dst, small_sem.at[i])
        for i, (src, dst) in enumerate((
            (ro_any, ro_ref), (mask_any, mask_ref), (len_any, len_ref), (gid_any, gid_ref)))
    ]
    for copy in small:
        copy.start()
    for q in (2, 3, 0, 1):
        own_copy(q).start()
    hid_copy = pltpu.make_async_copy(hid_any, hid, hid_sem)
    hid_copy.start()
    pl.semaphore_wait(barrier, n - 1 + plane - 1)

    send_own(0, inward)

    @pl.when(inner)
    def _():
        send_own(0, outward)

    for copy in small:
        copy.wait()
    r_copy().start()

    place = lax.broadcasted_iota(jnp.int32, (8, tok), 1)
    seq = lax.broadcasted_iota(jnp.int32, (8, tok), 0)
    inside = jnp.zeros((8, tok), jnp.bool_)
    start = jnp.int32(0)
    n_seq = len_any.shape[1]
    for j in range(n_seq):
        finish = start + len_ref[0, j]
        inside = inside | ((seq == j) & (place >= start) & (place < finish))
        start = finish
    member[...] = inside.astype(jnp.float32) * mask_ref[...].astype(jnp.float32)

    def weigh():
        line = lax.broadcasted_iota(jnp.int32, (8, qw), 0)
        total = jnp.zeros((8, rows), jnp.float32)
        for q in (2, 3, 0, 1):
            if q == 0:
                r_copy().wait_recv()
            own_copy(q).wait()
            values = (ro_ref if q >= 2 else robuf)[:, (q % 2) * qw:(q % 2 + 1) * qw]
            rest = jnp.broadcast_to(values, (8, qw))
            digits = jnp.zeros((8, qw), jnp.float32)
            for k in range(3):
                digit = rest.astype(jnp.bfloat16).astype(jnp.float32)
                digits = jnp.where(line == k, digit, digits)
                rest = rest - digit
            total += lax.dot_general(
                digits.astype(jnp.bfloat16), wbuf[q, block_at(f), :],
                (((1,), (1,)), ((), ())), preferred_element_type=jnp.float32)
        total = jnp.sum(total, axis=0, keepdims=True)
        for i in range(rows // 128):
            vbuf[f, i:i + 1, :] = total[:, i * 128:(i + 1) * 128]
        for k in range(1, n):
            v_copy(k, f).start()

    def gather_tokens():
        chosen = member[...].astype(jnp.bfloat16)
        step = 512 if depth % 512 == 0 else 128

        def part(i):
            at = pl.ds(pl.multiple_of(i * step, step), step)
            gsum[:, at] = jnp.dot(chosen, hid[:, at], preferred_element_type=jnp.float32)

        each(0, depth // step, part)

    def score():
        for k in range(1, n):
            v_copy(k, lax.rem(f + k, n)).wait_recv()
        total = jnp.zeros((8, 128), jnp.float32)
        for j in range(n):
            for i in range(rows // 128):
                at = j * rows + i * 128
                total += gsum[:, at:at + 128] * vbuf[j, i:i + 1, :]
        sbuf[me] = jnp.broadcast_to(jnp.sum(total, axis=1, keepdims=True), (8, 128))
        each(1, plane, lambda k: s_copy(k, me).start())

    row = lax.broadcasted_iota(jnp.int32, (8, 128), 0)
    lane = lax.broadcasted_iota(jnp.int32, (8, 128), 1)

    def reward():
        count = jnp.sum(member[...], axis=1, keepdims=True)
        each(1, plane, lambda k: s_copy(k, lax.rem(me + k, plane)).wait_recv())
        seq_sum = jnp.sum(sbuf[...], axis=0)
        row_gid = jnp.full((8, 128), -1, jnp.int32)
        for j in range(n_seq):
            row_gid = jnp.where(row == j, gid_ref[j], row_gid)
        zbuf[f, 0] = seq_sum / jnp.sqrt(jnp.maximum(count, 1.0))
        zbuf[f, 1] = row_gid.astype(jnp.float32)
        each(1, n, lambda k: z_copy(k, f).start())

    def advantage():
        each(1, n, lambda k: z_copy(k, lax.rem(f + k, n)).wait_recv())
        lane_gid = jnp.full((8, 128), -2, jnp.int32)
        for j in range(n_seq):
            lane_gid = jnp.where(lane == j, gid_ref[j], lane_gid)
        mine = jnp.sum(jnp.where(row == lane, zbuf[f, 0], 0.0), axis=0, keepdims=True)
        same = (zbuf[:, 1] == lane_gid.astype(jnp.float32)[None]).astype(jnp.float32)
        rewards = zbuf[:, 0]

        def over(value):
            return jnp.sum(jnp.sum(value, axis=0), axis=0, keepdims=True)

        size = jnp.maximum(over(same), 1.0)
        mean = over(same * rewards) / size
        var = over(same * (rewards - mean[None]) ** 2) / size
        adv_ref[...] = ((mine - mean) / jnp.sqrt(var + 1.0))[:, :n_seq]

    def add(q, at_depth, first=False, send=False, low=0, high=tiles):
        def product(i):
            at = tile_at(i)
            part = jnp.dot(
                hid[at, at_depth], wbuf[q, at_depth, :], preferred_element_type=jnp.float32)
            acc[q, at, :] = part if first else acc[q, at, :] + part
            if send:
                x_copy(q, i).start()

        each(low, high, product)

    whole = slice(None)

    def out_at(q):
        return slice((q - 2) * qw, (q - 1) * qw)

    def finish(q, at_depth):
        def product(i):
            at = tile_at(i)
            x_copy(q - 2, i).wait_recv()
            part = jnp.dot(
                hid[at, at_depth], wbuf[q, at_depth, :], preferred_element_type=jnp.float32)
            kv_ref[at, out_at(q)] = (acc[q, at, :] + precv[q - 2, at, :] + part).astype(jnp.bfloat16)

        each(0, tiles, product)

    def spread(i):
        h_recv(i, t).wait_recv()
        h_spread(0, i).start()
        h_spread(1, i).start()

    def relay(i):
        h_recv(i, across).wait_recv()
        h_spread(2, i).start()

    def partial(i):
        h_recv(i, mate).wait_recv()
        h_recv(i, cross).wait_recv()
        at = blk_at(i)
        racc[0, at, :] = jnp.dot(hbuf[at, :], wbuf[0, far, :], preferred_element_type=jnp.float32)
        q_copy(i).start()

    def give_back(i):
        at = blk_at(i)
        part = jnp.dot(hbuf[at, :], wbuf[2, far, :], preferred_element_type=jnp.float32)
        q_copy(i).wait_recv()
        racc[1, at, :] = part + rx[at, :]
        b_copy(i).start()

    def returned(i):
        at = blk_at(i)
        b_copy(i).wait_recv()
        kv_ref[at, out_at(2)] = (acc[2, at, :] + precv[0, at, :] + rret[at, :]).astype(jnp.bfloat16)

    weigh()

    @pl.when(outer)
    def _():
        mid, away, end = f + inward, f + 2 * inward, f + 3 * inward
        send_own(1, inward)
        send_own(2, inward)
        hid_copy.wait()
        each(0, 5, lambda i: h_copy(i).start())
        for r in range(parts):
            w_copy(3, f, r, inward, own=True).start()
            h_copy(5 + r).start()
        each(5 + parts, blocks, lambda i: h_copy(i).start())
        gather_tokens()
        take(0, mid)
        add(0, near, first=True, send=True)
        score()
        for q in range(1, 4):
            take(q, mid)
            add(q, near, first=True)
        reward()
        take(1, away)
        take(1, end)
        add(1, far, send=True)
        take(3, away)
        add(3, block_at(away))
        each(0, tiles, lambda i: x_copy(0, i).wait_recv())
        each(0, 5, returned)
        take(3, end, high=parts - 1)
        for r in range(parts - 1):
            add(3, depth_at(end, r))
        take(3, end, low=parts - 1)
        finish(3, depth_at(end, parts - 1))
        advantage()
        each(5, blocks, returned)

    @pl.when(inner)
    def _():
        edge, away, end = f + outward, f + inward, f + 2 * inward
        for q in range(1, 4):
            send_own(q, outward)
        for r in range(parts):
            take(0, edge, inward, low=r, high=r + 1)
            w_copy(1, f, r, inward, own=True).start()
        hid_copy.wait()
        gather_tokens()
        take(1, edge, inward)
        send_own(3, inward)
        take(0, away)
        take(0, end)
        score()
        add(0, whole, first=True, send=True)
        take(2, edge, inward)
        send_own(2, inward)
        take(1, away, outward)
        add(1, near, first=True)
        spread(0)
        take(1, end, outward)
        reward()
        spread(1)
        add(1, far, send=True, high=tiles // 2)
        relay(0)
        spread(2)
        partial(0)
        spread(3)
        relay(1)
        partial(1)
        take(3, away, outward)
        add(1, far, send=True, low=tiles // 2, high=tiles - 1)
        relay(2)
        spread(4)
        partial(2)
        relay(3)
        partial(3)
        take(3, edge, inward, high=1)
        add(2, near, first=True)
        relay(4)
        spread(5)
        partial(4)
        take(2, end)
        take(2, away)
        each(0, 5, give_back)
        take(3, edge, inward, low=1)
        relay(5)
        spread(6)
        partial(5)
        add(1, far, send=True, low=tiles - 1)
        take(3, end, outward, high=1)
        spread(7)
        take(3, end, outward, low=1)
        finish(2, far)
        relay(6)
        partial(6)
        give_back(5)
        relay(7)
        partial(7)
        give_back(6)
        add(3, near, first=True)
        give_back(7)
        advantage()
        finish(3, far)

    for q in range(2):
        each(0, tiles, lambda i: x_copy(q, i).wait_send())
    r_copy().wait_send()
    for k in range(1, n):
        v_copy(k, f).wait_send()
    each(1, plane, lambda k: s_copy(k, me).wait_send())
    each(1, n, lambda k: z_copy(k, f).wait_send())
    for r in range(parts):
        for q in range(4):
            w_copy(q, f, r, inward).wait_send()

    @pl.when(outer)
    def _():
        each(0, blocks, lambda i: h_copy(i).wait_send())

    @pl.when(inner)
    def _():
        for r in range(parts):
            for q in range(4):
                w_copy(q, f, r, outward).wait_send()
                w_copy(q, f + outward, r, inward).wait_send()
                if q % 2:
                    w_copy(q, f + inward, r, outward).wait_send()
                    w_copy(q, f + 2 * inward, r, outward).wait_send()

        def sent(i):
            for k in range(3):
                h_spread(k, i).wait_send()
            q_copy(i).wait_send()
            b_copy(i).wait_send()

        each(0, blocks, sent)


def solution(mesh):
    n, nt, ns = mesh.shape["fsdp"], mesh.shape["tp"], mesh.shape["sect"]

    def local(hidden, kv_weight, readout, lengths, prompt_mask, group_ids):
        tok, depth = hidden.shape
        rows, width = kv_weight.shape
        parts = max(1, min(2, rows // 256))
        cw = width // 2
        plane = nt * ns
        n_seq = lengths.shape[1]
        tile = min(256, tok)
        in_line = n == 4 and nt == 4 and ns == 2 and rows % 1024 == 0 and cw % 256 == 0 and tok % 1024 == 0
        dma = pltpu.SemaphoreType.DMA
        vmem, smem, anywhere = (
            pl.BlockSpec(memory_space=pltpu.VMEM),
            pl.BlockSpec(memory_space=pltpu.SMEM),
            pl.BlockSpec(memory_space=pl.ANY),
        )
        if in_line:
            blocks = 8
            body = functools.partial(line_kernel, nt, ns, parts, tile, blocks)
            tiles = tok // tile
            qw = cw // 2
            specs = [anywhere] * 6
            scratch = [
                pltpu.VMEM((1, cw), jnp.float32),
                pltpu.VMEM((1, tok), jnp.int32),
                pltpu.SMEM((1, n_seq), jnp.int32),
                pltpu.SMEM((n_seq,), jnp.int32),
                dma((4,)),
                pltpu.VMEM((tok, depth), jnp.bfloat16),
                pltpu.VMEM((4, depth, qw), jnp.bfloat16),
                pltpu.VMEM((4, tok, qw), jnp.float32),
                pltpu.VMEM((2, tok, qw), jnp.float32),
                pltpu.VMEM((tok, 2 * rows), jnp.bfloat16),
                pltpu.VMEM((2, tok, qw), jnp.float32),
                pltpu.VMEM((tok, qw), jnp.float32),
                pltpu.VMEM((tok, qw), jnp.float32),
                pltpu.VMEM((8, tok), jnp.float32),
                pltpu.VMEM((8, depth), jnp.float32),
                pltpu.VMEM((1, cw), jnp.float32),
                pltpu.VMEM((n, rows // 128, 128), jnp.float32),
                pltpu.VMEM((plane, 8, 128), jnp.float32),
                pltpu.VMEM((n, 2, 8, 128), jnp.float32),
                dma, dma((4,)),
                dma((2, 4, parts, n)), dma((4, parts, n)),
                dma((2, tiles)), dma((2, tiles)),
                dma, dma,
                dma((n,)), dma((n,)),
                dma((plane,)), dma((plane,)),
                dma((n,)), dma((n,)),
                dma((3, blocks)), dma((blocks, nt)),
                dma((blocks,)), dma((blocks,)),
                dma((blocks,)), dma((blocks,)),
            ]
        else:
            body = functools.partial(kernel, n, nt, ns, parts, tile)
            specs = [anywhere, anywhere, vmem, vmem, smem, smem]
            scratch = [
                pltpu.VMEM((tok, depth), jnp.bfloat16),
                pltpu.VMEM((2, depth, cw), jnp.bfloat16),
                pltpu.VMEM((2, tok, cw), jnp.float32),
                pltpu.VMEM((tok, cw), jnp.float32),
                pltpu.VMEM((8, tok), jnp.float32),
                pltpu.VMEM((plane, 8, cw), jnp.float32),
                pltpu.VMEM((n, 2, 8, 128), jnp.float32),
                dma, dma((2, parts)),
                dma((2, 2, parts, n)), dma((2, parts, n)),
                dma, dma,
                dma((plane,)), dma((plane,)),
                dma((n,)), dma((n,)),
            ]
        kv, adv = pl.pallas_call(
            body,
            out_shape=(
                pltpu.VMEM((tok, width // 2), jnp.bfloat16),
                pltpu.VMEM((1, n_seq), jnp.float32),
            ),
            in_specs=specs,
            out_specs=(vmem, vmem),
            scratch_shapes=scratch,
            compiler_params=pltpu.CompilerParams(collective_id=0, has_side_effects=True),
        )(hidden, kv_weight, readout[None, :], prompt_mask[None, :], lengths, group_ids)
        return kv, adv[0]

    return jax.shard_map(
        local,
        mesh=mesh,
        in_specs=(
            P("fsdp", "sect"),
            P(("sect", "fsdp"), "tp"),
            P(("tp", "sect")),
            P("fsdp", None),
            P("fsdp"),
            P("fsdp"),
        ),
        out_specs=(P("fsdp", ("tp", "sect")), P("fsdp")),
        check_vma=False,
    )
```

```python
import functools

import jax
import jax.numpy as jnp
from jax import lax
from jax.experimental import pallas as pl
from jax.experimental.pallas import tpu as pltpu
from jax.sharding import PartitionSpec as P

MESH = pl.DeviceIdType.MESH


def kernel(
    n, nt, ns, parts, tile,
    hid_any, w_any, ro_ref, mask_ref, len_ref, gid_ref,
    kv_ref, adv_ref,
    hid, wbuf, acc, precv, member, sbuf, zbuf,
    hid_sem, own_sem, wsend, wrecv, xsend, xrecv, ssend, srecv, zsend, zrecv,
):
    f, t, s = lax.axis_index("fsdp"), lax.axis_index("tp"), lax.axis_index("sect")
    plane = nt * ns
    me = t * ns + s
    rows, width = w_any.shape
    cw = width // 2
    piece = rows // parts
    by_piece = piece % 128 == 0
    tok = hid.shape[0]

    def plane_id(k):
        other = lax.rem(me + k, plane)
        return {"tp": lax.div(other, ns), "sect": lax.rem(other, ns)}

    def line_id(k):
        return {"fsdp": lax.rem(f + k, n)}

    def cols(c):
        side = s if c else 1 - s
        return pl.ds(pl.multiple_of(side * cw, cw), cw)

    def depth_at(j, r):
        return pl.ds(pl.multiple_of(j * rows + r * piece, piece), piece)

    def own_rows(c, r):
        return w_any.at[r * piece:(r + 1) * piece, cols(c)]

    def w_copy(c, j, r, step, own):
        place = wbuf.at[c, depth_at(j, r), :]
        return pltpu.make_async_remote_copy(
            src_ref=own_rows(c, r) if own else place,
            dst_ref=place,
            send_sem=wsend.at[0 if step > 0 else 1, c, r, j],
            recv_sem=wrecv.at[c, r, j],
            device_id={"fsdp": f + step},
            device_id_type=MESH,
        )

    def x_copy():
        return pltpu.make_async_remote_copy(
            src_ref=acc.at[0],
            dst_ref=precv,
            send_sem=xsend,
            recv_sem=xrecv,
            device_id={"sect": 1 - s},
            device_id_type=MESH,
        )

    def s_copy(k, slot):
        return pltpu.make_async_remote_copy(
            src_ref=sbuf.at[slot],
            dst_ref=sbuf.at[slot],
            send_sem=ssend.at[k],
            recv_sem=srecv.at[slot],
            device_id=plane_id(k),
            device_id_type=MESH,
        )

    def z_copy(k, slot):
        return pltpu.make_async_remote_copy(
            src_ref=zbuf.at[slot],
            dst_ref=zbuf.at[slot],
            send_sem=zsend.at[k],
            recv_sem=zrecv.at[slot],
            device_id=line_id(k),
            device_id_type=MESH,
        )

    def each(low, high, body):
        def step(i, carry):
            body(i)
            return carry

        lax.fori_loop(low, high, step, 0)

    barrier = pltpu.get_barrier_semaphore()
    each(1, n, lambda k: pl.semaphore_signal(
        barrier, inc=1, device_id=line_id(k), device_id_type=MESH))
    each(1, plane, lambda k: pl.semaphore_signal(
        barrier, inc=1, device_id=plane_id(k), device_id_type=MESH))

    def own_copy(c, r):
        return pltpu.make_async_copy(
            own_rows(c, r), wbuf.at[c, depth_at(f, r), :], own_sem.at[c, r])

    def send_own(c, step):
        for r in range(parts):
            w_copy(c, f, r, step, True).start()

    pl.semaphore_wait(barrier, n - 1 + plane - 1)

    @pl.when(f < n - 1)
    def _():
        send_own(0, 1)

    @pl.when(f > 0)
    def _():
        send_own(0, -1)

    @pl.when(f == 0)
    def _():
        send_own(1, 1)

    @pl.when(f == n - 1)
    def _():
        send_own(1, -1)

    hid_copy = pltpu.make_async_copy(hid_any, hid, hid_sem)
    for c in range(2):
        for r in range(parts):
            own_copy(c, r).start()
    hid_copy.start()

    place = lax.broadcasted_iota(jnp.int32, (8, tok), 1)
    seq = lax.broadcasted_iota(jnp.int32, (8, tok), 0)
    inside = jnp.zeros((8, tok), jnp.bool_)
    start = jnp.int32(0)
    n_seq = len_ref.shape[1]
    for j in range(n_seq):
        finish = start + len_ref[0, j]
        inside = inside | ((seq == j) & (place >= start) & (place < finish))
        start = finish
    member[...] = inside.astype(jnp.float32) * mask_ref[...].astype(jnp.float32)

    def add(c, depth, first):
        def product(i, carry):
            at = pl.ds(pl.multiple_of(i * tile, tile), tile)
            part = jnp.dot(
                hid[at, depth], wbuf[c, depth, :], preferred_element_type=jnp.float32)
            acc[c, at, :] = part if first else acc[c, at, :] + part
            return carry

        lax.fori_loop(0, tok // tile, product, 0)

    def arrive(c, j, r, step):
        w_copy(c, j, r, -step, False).wait_recv()

        @pl.when((f + step >= 0) & (f + step < n))
        def _():
            w_copy(c, j, r, step, False).start()

        if by_piece:
            add(c, depth_at(j, r), False)

    for c in range(2):
        for r in range(parts):
            own_copy(c, r).wait()
        if c == 0:
            hid_copy.wait()
        if by_piece:
            add(c, pl.ds(pl.multiple_of(f * rows, rows), rows), True)

        def visit(d, c=c):
            left, right = f - d, f + d
            for r in range(parts):
                @pl.when(left >= 0)
                def _():
                    arrive(c, left, r, 1)

                @pl.when(right < n)
                def _():
                    arrive(c, right, r, -1)

            if c == 0:
                @pl.when((d == f) & (f < n - 1))
                def _():
                    send_own(1, 1)

                @pl.when((d == n - 1 - f) & (f > 0))
                def _():
                    send_own(1, -1)

        each(1, n, visit)
        if not by_piece:
            add(c, slice(None), True)
        if c == 0:
            x_copy().start()

    x_copy().wait_recv()

    def finish_rows(i, carry):
        at = pl.ds(pl.multiple_of(i * tile, tile), tile)
        projected = acc[1, at, :] + precv[at, :]
        kv_ref[at, :] = projected.astype(jnp.bfloat16)
        chosen = member[:, at].astype(jnp.bfloat16)
        rest = projected
        for _ in range(3):
            digits = rest.astype(jnp.bfloat16)
            carry += jnp.dot(chosen, digits, preferred_element_type=jnp.float32)
            rest = rest - digits.astype(jnp.float32)
        return carry

    total = lax.fori_loop(
        0, tok // tile, finish_rows, jnp.zeros((8, cw), jnp.float32)) * ro_ref[...]
    sbuf[me] = total
    each(1, plane, lambda k: s_copy(k, me).start())
    count = jnp.sum(member[...], axis=1, keepdims=True)
    each(1, plane, lambda k: s_copy(k, lax.rem(me + k, plane)).wait_recv())
    seq_sum = jnp.sum(jnp.sum(sbuf[...], axis=0), axis=1, keepdims=True)
    reward = seq_sum / jnp.sqrt(jnp.maximum(count, 1.0))

    row = lax.broadcasted_iota(jnp.int32, (8, 128), 0)
    lane = lax.broadcasted_iota(jnp.int32, (8, 128), 1)
    row_gid = jnp.full((8, 128), -1, jnp.int32)
    lane_gid = jnp.full((8, 128), -2, jnp.int32)
    for j in range(n_seq):
        row_gid = jnp.where(row == j, gid_ref[j], row_gid)
        lane_gid = jnp.where(lane == j, gid_ref[j], lane_gid)
    reward = jnp.broadcast_to(reward, (8, 128))
    zbuf[f, 0] = reward
    zbuf[f, 1] = row_gid.astype(jnp.float32)
    each(1, n, lambda k: z_copy(k, f).start())
    mine = jnp.sum(jnp.where(row == lane, reward, 0.0), axis=0, keepdims=True)
    each(1, n, lambda k: z_copy(k, lax.rem(f + k, n)).wait_recv())
    same = (zbuf[:, 1] == lane_gid.astype(jnp.float32)[None]).astype(jnp.float32)
    rewards = zbuf[:, 0]

    def over(value):
        return jnp.sum(jnp.sum(value, axis=0), axis=0, keepdims=True)

    size = jnp.maximum(over(same), 1.0)
    mean = over(same * rewards) / size
    var = over(same * (rewards - mean[None]) ** 2) / size
    adv_ref[...] = ((mine - mean) / jnp.sqrt(var + 1.0))[:, :n_seq]

    each(1, plane, lambda k: s_copy(k, me).wait_send())
    each(1, n, lambda k: z_copy(k, f).wait_send())
    x_copy().wait_send()
    for c in range(2):
        def sent(j, c=c):
            for r in range(parts):
                @pl.when((j <= f) & (f < n - 1))
                def _():
                    w_copy(c, j, r, 1, False).wait_send()

                @pl.when((j >= f) & (f > 0))
                def _():
                    w_copy(c, j, r, -1, False).wait_send()

        each(0, n, sent)


def line_kernel(
    nt, ns, parts, tile, blocks,
    hid_any, w_any, ro_any, mask_any, len_any, gid_any,
    kv_ref, adv_ref,
    ro_ref, mask_ref, len_ref, gid_ref, small_sem,
    hid, wbuf, acc, precv, hbuf, racc, rx, rret, member, gsum, robuf, vbuf, sbuf, zbuf,
    hid_sem, own_sem, wsend, wrecv, xsend, xrecv, rsend, rrecv,
    vsend, vrecv, ssend, srecv, zsend, zrecv,
    hsend, hrecv, qsend, qrecv, bsend, brecv, line_in, plane_in,
):
    n = 4
    f, t, s = lax.axis_index("fsdp"), lax.axis_index("tp"), lax.axis_index("sect")
    plane = nt * ns
    me = t * ns + s
    rows, width = w_any.shape
    cw = width // 2
    qw = cw // 2
    piece = rows // parts
    tok, depth = hid.shape
    tiles = tok // tile
    blk = tok // blocks
    share = blk // nt
    inward = jnp.where(f < 2, 1, -1)
    outward = -inward
    outer = (f == 0) | (f == n - 1)
    inner = (f == 1) | (f == n - 2)
    near_at = jnp.where(f < 2, 0, 2 * rows)
    near = pl.ds(pl.multiple_of(near_at, rows), 2 * rows)
    far = pl.ds(pl.multiple_of(2 * rows - near_at, rows), 2 * rows)
    mate = lax.div(t, 2) * 2 + (1 - lax.rem(t, 2))
    across = lax.rem(t + 2, 4)
    cross = lax.rem(mate + 2, 4)

    def plane_id(k):
        other = lax.rem(me + k, plane)
        return {"tp": lax.div(other, ns), "sect": lax.rem(other, ns)}

    def line_id(k):
        return {"fsdp": lax.rem(f + k, n)}

    def cols(q):
        side = s if q >= 2 else 1 - s
        return pl.ds(pl.multiple_of(side * cw + (q % 2) * qw, qw), qw)

    def depth_at(j, r):
        return pl.ds(pl.multiple_of(j * rows + r * piece, piece), piece)

    def block_at(j):
        return pl.ds(pl.multiple_of(j * rows, rows), rows)

    def tile_at(i):
        return pl.ds(pl.multiple_of(i * tile, tile), tile)

    def blk_at(i):
        return pl.ds(pl.multiple_of(i * blk, blk), blk)

    def share_at(i, p):
        return pl.ds(pl.multiple_of(i * blk + p * share, share), share)

    def remote(src, dst, send, recv, device):
        return pltpu.make_async_remote_copy(
            src_ref=src, dst_ref=dst, send_sem=send, recv_sem=recv,
            device_id=device, device_id_type=MESH)

    def w_copy(q, j, r, step, own=False):
        place = wbuf.at[q, depth_at(j, r), :]
        src = w_any.at[r * piece:(r + 1) * piece, cols(q)] if own else place
        toward = 0 if step is inward else 1
        return remote(src, place, wsend.at[toward, q, r, j], wrecv.at[q, r, j], {"fsdp": f + step})

    def x_copy(q, i):
        at = tile_at(i)
        return remote(acc.at[q, at], precv.at[q, at], xsend.at[q, i], xrecv.at[q, i], {"sect": 1 - s})

    def h_copy(i):
        at = share_at(i, t)
        return remote(hid.at[at, far], hbuf.at[at], hsend.at[0, i], hrecv.at[i, t], {"fsdp": f + inward})

    def h_spread(k, i):
        p = (t, t, across)[k]
        to = (mate, across, mate)[k]
        at = share_at(i, p)
        return remote(hbuf.at[at], hbuf.at[at], hsend.at[k, i], hrecv.at[i, p], {"tp": to})

    def h_recv(i, p):
        at = share_at(i, p)
        return remote(hbuf.at[at], hbuf.at[at], hsend.at[0, i], hrecv.at[i, p], {"tp": mate})

    def q_copy(i):
        at = blk_at(i)
        return remote(racc.at[0, at], rx.at[at], qsend.at[i], qrecv.at[i], {"sect": 1 - s})

    def b_copy(i):
        at = blk_at(i)
        return remote(racc.at[1, at], rret.at[at], bsend.at[i], brecv.at[i], {"fsdp": f + outward})

    def r_copy():
        return remote(ro_ref, robuf, rsend, rrecv, {"sect": 1 - s})

    def v_copy(k, slot):
        return remote(vbuf.at[slot], vbuf.at[slot], vsend.at[k], vrecv.at[slot], line_id(k))

    def s_copy(k, slot):
        return remote(sbuf.at[slot], sbuf.at[slot], ssend.at[k], srecv.at[slot], plane_id(k))

    def z_copy(k, slot):
        return remote(zbuf.at[slot], zbuf.at[slot], zsend.at[k], zrecv.at[slot], line_id(k))

    def own_copy(q):
        return pltpu.make_async_copy(
            w_any.at[:, cols(q)], wbuf.at[q, block_at(f), :], own_sem.at[q])

    def each(low, high, body):
        def step(i, carry):
            body(i)
            return carry

        lax.fori_loop(low, high, step, 0)

    def send_own(q, step):
        for r in range(parts):
            w_copy(q, f, r, step, own=True).start()

    def take(q, j, step=None, low=0, high=parts):
        for r in range(low, high):
            w_copy(q, j, r, outward).wait_recv()
            if step is not None:
                w_copy(q, j, r, step).start()

    def tell(semaphore, device):
        pl.semaphore_signal(semaphore, inc=1, device_id=device, device_id_type=MESH)

    barrier = pltpu.get_barrier_semaphore()
    beside = ({"sect": 1 - s}, {"tp": across}, {"tp": mate})
    tell(barrier, {"fsdp": f + inward})

    @pl.when(inner)
    def _():
        tell(barrier, {"fsdp": f + outward})

    for device in beside:
        tell(barrier, device)
    small = [
        pltpu.make_async_copy(src, dst, small_sem.at[i])
        for i, (src, dst) in enumerate((
            (ro_any, ro_ref), (mask_any, mask_ref), (len_any, len_ref), (gid_any, gid_ref)))
    ]
    for copy in small:
        copy.start()
    for q in (2, 3, 0, 1):
        own_copy(q).start()
    hid_copy = pltpu.make_async_copy(hid_any, hid, hid_sem)
    hid_copy.start()
    pl.semaphore_wait(barrier, jnp.where(outer, 4, 5))

    send_own(0, inward)

    @pl.when(inner)
    def _():
        send_own(0, outward)
        tell(line_in.at[0], {"fsdp": f + inward})
        tell(line_in.at[0], {"fsdp": f + outward})

    for device in beside:
        tell(plane_in.at[0], device)
    for copy in small:
        copy.wait()
    r_copy().start()

    place = lax.broadcasted_iota(jnp.int32, (8, tok), 1)
    seq = lax.broadcasted_iota(jnp.int32, (8, tok), 0)
    inside = jnp.zeros((8, tok), jnp.bool_)
    start = jnp.int32(0)
    n_seq = len_any.shape[1]
    for j in range(n_seq):
        finish = start + len_ref[0, j]
        inside = inside | ((seq == j) & (place >= start) & (place < finish))
        start = finish
    member[...] = inside.astype(jnp.float32) * mask_ref[...].astype(jnp.float32)

    def weigh():
        line = lax.broadcasted_iota(jnp.int32, (8, qw), 0)
        total = jnp.zeros((8, rows), jnp.float32)
        for q in (2, 3, 0, 1):
            if q == 0:
                r_copy().wait_recv()
            own_copy(q).wait()
            values = (ro_ref if q >= 2 else robuf)[:, (q % 2) * qw:(q % 2 + 1) * qw]
            rest = jnp.broadcast_to(values, (8, qw))
            digits = jnp.zeros((8, qw), jnp.float32)
            for k in range(3):
                digit = rest.astype(jnp.bfloat16).astype(jnp.float32)
                digits = jnp.where(line == k, digit, digits)
                rest = rest - digit
            total += lax.dot_general(
                digits.astype(jnp.bfloat16), wbuf[q, block_at(f), :],
                (((1,), (1,)), ((), ())), preferred_element_type=jnp.float32)
        total = jnp.sum(total, axis=0, keepdims=True)
        for i in range(rows // 128):
            vbuf[f, i:i + 1, :] = total[:, i * 128:(i + 1) * 128]
        pl.semaphore_wait(plane_in.at[0], 3)
        tell(plane_in.at[1], {"sect": 1 - s})
        pl.semaphore_wait(line_in.at[0], 1)

        @pl.when(inner)
        def _():
            tell(line_in.at[1], {"fsdp": f + outward})

        @pl.when(outer)
        def _():
            pl.semaphore_wait(line_in.at[1], 1)

        for k in range(1, n):
            v_copy(k, f).start()

    def gather_tokens():
        chosen = member[...].astype(jnp.bfloat16)
        step = 512 if depth % 512 == 0 else 128

        def part(i):
            at = pl.ds(pl.multiple_of(i * step, step), step)
            gsum[:, at] = jnp.dot(chosen, hid[:, at], preferred_element_type=jnp.float32)

        each(0, depth // step, part)

    def score():
        for k in range(1, n):
            v_copy(k, lax.rem(f + k, n)).wait_recv()
        total = jnp.zeros((8, 128), jnp.float32)
        for j in range(n):
            for i in range(rows // 128):
                at = j * rows + i * 128
                total += gsum[:, at:at + 128] * vbuf[j, i:i + 1, :]
        sbuf[me] = jnp.broadcast_to(jnp.sum(total, axis=1, keepdims=True), (8, 128))
        pl.semaphore_wait(plane_in.at[1], 1)
        each(1, plane, lambda k: s_copy(k, me).start())

    row = lax.broadcasted_iota(jnp.int32, (8, 128), 0)
    lane = lax.broadcasted_iota(jnp.int32, (8, 128), 1)

    def reward():
        count = jnp.sum(member[...], axis=1, keepdims=True)
        each(1, plane, lambda k: s_copy(k, lax.rem(me + k, plane)).wait_recv())
        seq_sum = jnp.sum(sbuf[...], axis=0)
        row_gid = jnp.full((8, 128), -1, jnp.int32)
        for j in range(n_seq):
            row_gid = jnp.where(row == j, gid_ref[j], row_gid)
        zbuf[f, 0] = seq_sum / jnp.sqrt(jnp.maximum(count, 1.0))
        zbuf[f, 1] = row_gid.astype(jnp.float32)
        each(1, n, lambda k: z_copy(k, f).start())

    def advantage():
        each(1, n, lambda k: z_copy(k, lax.rem(f + k, n)).wait_recv())
        lane_gid = jnp.full((8, 128), -2, jnp.int32)
        for j in range(n_seq):
            lane_gid = jnp.where(lane == j, gid_ref[j], lane_gid)
        mine = jnp.sum(jnp.where(row == lane, zbuf[f, 0], 0.0), axis=0, keepdims=True)
        same = (zbuf[:, 1] == lane_gid.astype(jnp.float32)[None]).astype(jnp.float32)
        rewards = zbuf[:, 0]

        def over(value):
            return jnp.sum(jnp.sum(value, axis=0), axis=0, keepdims=True)

        size = jnp.maximum(over(same), 1.0)
        mean = over(same * rewards) / size
        var = over(same * (rewards - mean[None]) ** 2) / size
        adv_ref[...] = ((mine - mean) / jnp.sqrt(var + 1.0))[:, :n_seq]

    def add(q, at_depth, first=False, send=False, low=0, high=tiles):
        def product(i):
            at = tile_at(i)
            part = jnp.dot(
                hid[at, at_depth], wbuf[q, at_depth, :], preferred_element_type=jnp.float32)
            acc[q, at, :] = part if first else acc[q, at, :] + part
            if send:
                x_copy(q, i).start()

        each(low, high, product)

    whole = slice(None)

    def out_at(q):
        return slice((q - 2) * qw, (q - 1) * qw)

    def finish(q, at_depth):
        def product(i):
            at = tile_at(i)
            x_copy(q - 2, i).wait_recv()
            part = jnp.dot(
                hid[at, at_depth], wbuf[q, at_depth, :], preferred_element_type=jnp.float32)
            kv_ref[at, out_at(q)] = (acc[q, at, :] + precv[q - 2, at, :] + part).astype(jnp.bfloat16)

        each(0, tiles, product)

    def spread(i):
        h_recv(i, t).wait_recv()
        h_spread(0, i).start()
        h_spread(1, i).start()

    def relay(i):
        h_recv(i, across).wait_recv()
        h_spread(2, i).start()

    def partial(i):
        h_recv(i, mate).wait_recv()
        h_recv(i, cross).wait_recv()
        at = blk_at(i)
        racc[0, at, :] = jnp.dot(hbuf[at, :], wbuf[0, far, :], preferred_element_type=jnp.float32)
        q_copy(i).start()

    def give_back(i):
        at = blk_at(i)
        part = jnp.dot(hbuf[at, :], wbuf[2, far, :], preferred_element_type=jnp.float32)
        q_copy(i).wait_recv()
        racc[1, at, :] = part + rx[at, :]
        b_copy(i).start()

    def returned(i):
        at = blk_at(i)
        b_copy(i).wait_recv()
        kv_ref[at, out_at(2)] = (acc[2, at, :] + precv[0, at, :] + rret[at, :]).astype(jnp.bfloat16)

    weigh()

    @pl.when(outer)
    def _():
        mid, away, end = f + inward, f + 2 * inward, f + 3 * inward
        send_own(1, inward)
        send_own(2, inward)
        hid_copy.wait()
        each(0, 5, lambda i: h_copy(i).start())
        for r in range(parts):
            w_copy(3, f, r, inward, own=True).start()
            h_copy(5 + r).start()
        each(5 + parts, blocks, lambda i: h_copy(i).start())
        gather_tokens()
        take(0, mid)
        add(0, near, first=True, send=True)
        score()
        for q in range(1, 4):
            take(q, mid)
            add(q, near, first=True)
        reward()
        take(1, away)
        take(1, end)
        add(1, far, send=True)
        take(3, away)
        add(3, block_at(away))
        each(0, tiles, lambda i: x_copy(0, i).wait_recv())
        each(0, 5, returned)
        take(3, end, high=parts - 1)
        for r in range(parts - 1):
            add(3, depth_at(end, r))
        take(3, end, low=parts - 1)
        finish(3, depth_at(end, parts - 1))
        advantage()
        each(5, blocks, returned)

    @pl.when(inner)
    def _():
        edge, away, end = f + outward, f + inward, f + 2 * inward
        for q in range(1, 4):
            send_own(q, outward)
        for r in range(parts):
            take(0, edge, inward, low=r, high=r + 1)
            w_copy(1, f, r, inward, own=True).start()
        hid_copy.wait()
        gather_tokens()
        take(1, edge, inward)
        send_own(3, inward)
        take(0, away)
        take(0, end)
        score()
        add(0, whole, first=True, send=True)
        take(2, edge, inward)
        send_own(2, inward)
        take(1, away, outward)
        add(1, near, first=True)
        spread(0)
        take(1, end, outward)
        reward()
        spread(1)
        add(1, far, send=True, high=tiles // 2)
        relay(0)
        spread(2)
        partial(0)
        spread(3)
        relay(1)
        partial(1)
        take(3, away, outward)
        add(1, far, send=True, low=tiles // 2, high=tiles - 1)
        relay(2)
        spread(4)
        partial(2)
        relay(3)
        partial(3)
        take(3, edge, inward, high=1)
        add(2, near, first=True)
        relay(4)
        spread(5)
        partial(4)
        take(2, end)
        take(2, away)
        each(0, 5, give_back)
        take(3, edge, inward, low=1)
        relay(5)
        spread(6)
        partial(5)
        add(1, far, send=True, low=tiles - 1)
        take(3, end, outward, high=1)
        spread(7)
        take(3, end, outward, low=1)
        finish(2, far)
        relay(6)
        partial(6)
        give_back(5)
        relay(7)
        partial(7)
        give_back(6)
        add(3, near, first=True)
        give_back(7)
        advantage()
        finish(3, far)

    for q in range(2):
        each(0, tiles, lambda i: x_copy(q, i).wait_send())
    r_copy().wait_send()
    for k in range(1, n):
        v_copy(k, f).wait_send()
    each(1, plane, lambda k: s_copy(k, me).wait_send())
    each(1, n, lambda k: z_copy(k, f).wait_send())
    for r in range(parts):
        for q in range(4):
            w_copy(q, f, r, inward).wait_send()

    @pl.when(outer)
    def _():
        each(0, blocks, lambda i: h_copy(i).wait_send())

    @pl.when(inner)
    def _():
        for r in range(parts):
            for q in range(4):
                w_copy(q, f, r, outward).wait_send()
                w_copy(q, f + outward, r, inward).wait_send()
                if q % 2:
                    w_copy(q, f + inward, r, outward).wait_send()
                    w_copy(q, f + 2 * inward, r, outward).wait_send()

        def sent(i):
            for k in range(3):
                h_spread(k, i).wait_send()
            q_copy(i).wait_send()
            b_copy(i).wait_send()

        each(0, blocks, sent)


def solution(mesh):
    n, nt, ns = mesh.shape["fsdp"], mesh.shape["tp"], mesh.shape["sect"]

    def local(hidden, kv_weight, readout, lengths, prompt_mask, group_ids):
        tok, depth = hidden.shape
        rows, width = kv_weight.shape
        parts = max(1, min(2, rows // 256))
        cw = width // 2
        plane = nt * ns
        n_seq = lengths.shape[1]
        tile = min(256, tok)
        in_line = n == 4 and nt == 4 and ns == 2 and rows % 1024 == 0 and cw % 256 == 0 and tok % 1024 == 0
        dma = pltpu.SemaphoreType.DMA
        vmem, smem, anywhere = (
            pl.BlockSpec(memory_space=pltpu.VMEM),
            pl.BlockSpec(memory_space=pltpu.SMEM),
            pl.BlockSpec(memory_space=pl.ANY),
        )
        if in_line:
            blocks = 8
            body = functools.partial(line_kernel, nt, ns, parts, tile, blocks)
            tiles = tok // tile
            qw = cw // 2
            specs = [anywhere] * 6
            scratch = [
                pltpu.VMEM((1, cw), jnp.float32),
                pltpu.VMEM((1, tok), jnp.int32),
                pltpu.SMEM((1, n_seq), jnp.int32),
                pltpu.SMEM((n_seq,), jnp.int32),
                dma((4,)),
                pltpu.VMEM((tok, depth), jnp.bfloat16),
                pltpu.VMEM((4, depth, qw), jnp.bfloat16),
                pltpu.VMEM((4, tok, qw), jnp.float32),
                pltpu.VMEM((2, tok, qw), jnp.float32),
                pltpu.VMEM((tok, 2 * rows), jnp.bfloat16),
                pltpu.VMEM((2, tok, qw), jnp.float32),
                pltpu.VMEM((tok, qw), jnp.float32),
                pltpu.VMEM((tok, qw), jnp.float32),
                pltpu.VMEM((8, tok), jnp.float32),
                pltpu.VMEM((8, depth), jnp.float32),
                pltpu.VMEM((1, cw), jnp.float32),
                pltpu.VMEM((n, rows // 128, 128), jnp.float32),
                pltpu.VMEM((plane, 8, 128), jnp.float32),
                pltpu.VMEM((n, 2, 8, 128), jnp.float32),
                dma, dma((4,)),
                dma((2, 4, parts, n)), dma((4, parts, n)),
                dma((2, tiles)), dma((2, tiles)),
                dma, dma,
                dma((n,)), dma((n,)),
                dma((plane,)), dma((plane,)),
                dma((n,)), dma((n,)),
                dma((3, blocks)), dma((blocks, nt)),
                dma((blocks,)), dma((blocks,)),
                dma((blocks,)), dma((blocks,)),
                pltpu.SemaphoreType.REGULAR((2,)), pltpu.SemaphoreType.REGULAR((2,)),
            ]
        else:
            body = functools.partial(kernel, n, nt, ns, parts, tile)
            specs = [anywhere, anywhere, vmem, vmem, smem, smem]
            scratch = [
                pltpu.VMEM((tok, depth), jnp.bfloat16),
                pltpu.VMEM((2, depth, cw), jnp.bfloat16),
                pltpu.VMEM((2, tok, cw), jnp.float32),
                pltpu.VMEM((tok, cw), jnp.float32),
                pltpu.VMEM((8, tok), jnp.float32),
                pltpu.VMEM((plane, 8, cw), jnp.float32),
                pltpu.VMEM((n, 2, 8, 128), jnp.float32),
                dma, dma((2, parts)),
                dma((2, 2, parts, n)), dma((2, parts, n)),
                dma, dma,
                dma((plane,)), dma((plane,)),
                dma((n,)), dma((n,)),
            ]
        kv, adv = pl.pallas_call(
            body,
            out_shape=(
                pltpu.VMEM((tok, width // 2), jnp.bfloat16),
                pltpu.VMEM((1, n_seq), jnp.float32),
            ),
            in_specs=specs,
            out_specs=(vmem, vmem),
            scratch_shapes=scratch,
            compiler_params=pltpu.CompilerParams(collective_id=0, has_side_effects=True),
        )(hidden, kv_weight, readout[None, :], prompt_mask[None, :], lengths, group_ids)
        return kv, adv[0]

    return jax.shard_map(
        local,
        mesh=mesh,
        in_specs=(
            P("fsdp", "sect"),
            P(("sect", "fsdp"), "tp"),
            P(("tp", "sect")),
            P("fsdp", None),
            P("fsdp"),
            P("fsdp"),
        ),
        out_specs=(P("fsdp", ("tp", "sect")), P("fsdp")),
        check_vma=False,
    )
```

```python
import functools

import jax
import jax.numpy as jnp
from jax import lax
from jax.experimental import pallas as pl
from jax.experimental.pallas import tpu as pltpu
from jax.sharding import PartitionSpec as P

MESH = pl.DeviceIdType.MESH


def kernel(
    n, nt, ns, parts, tile,
    hid_any, w_any, ro_ref, mask_ref, len_ref, gid_ref,
    kv_ref, adv_ref,
    hid, wbuf, acc, precv, member, sbuf, zbuf,
    hid_sem, own_sem, wsend, wrecv, xsend, xrecv, ssend, srecv, zsend, zrecv,
):
    f, t, s = lax.axis_index("fsdp"), lax.axis_index("tp"), lax.axis_index("sect")
    plane = nt * ns
    me = t * ns + s
    rows, width = w_any.shape
    cw = width // 2
    piece = rows // parts
    by_piece = piece % 128 == 0
    tok = hid.shape[0]

    def plane_id(k):
        other = lax.rem(me + k, plane)
        return {"tp": lax.div(other, ns), "sect": lax.rem(other, ns)}

    def line_id(k):
        return {"fsdp": lax.rem(f + k, n)}

    def cols(c):
        side = s if c else 1 - s
        return pl.ds(pl.multiple_of(side * cw, cw), cw)

    def depth_at(j, r):
        return pl.ds(pl.multiple_of(j * rows + r * piece, piece), piece)

    def own_rows(c, r):
        return w_any.at[r * piece:(r + 1) * piece, cols(c)]

    def w_copy(c, j, r, step, own):
        place = wbuf.at[c, depth_at(j, r), :]
        return pltpu.make_async_remote_copy(
            src_ref=own_rows(c, r) if own else place,
            dst_ref=place,
            send_sem=wsend.at[0 if step > 0 else 1, c, r, j],
            recv_sem=wrecv.at[c, r, j],
            device_id={"fsdp": f + step},
            device_id_type=MESH,
        )

    def x_copy():
        return pltpu.make_async_remote_copy(
            src_ref=acc.at[0],
            dst_ref=precv,
            send_sem=xsend,
            recv_sem=xrecv,
            device_id={"sect": 1 - s},
            device_id_type=MESH,
        )

    def s_copy(k, slot):
        return pltpu.make_async_remote_copy(
            src_ref=sbuf.at[slot],
            dst_ref=sbuf.at[slot],
            send_sem=ssend.at[k],
            recv_sem=srecv.at[slot],
            device_id=plane_id(k),
            device_id_type=MESH,
        )

    def z_copy(k, slot):
        return pltpu.make_async_remote_copy(
            src_ref=zbuf.at[slot],
            dst_ref=zbuf.at[slot],
            send_sem=zsend.at[k],
            recv_sem=zrecv.at[slot],
            device_id=line_id(k),
            device_id_type=MESH,
        )

    def each(low, high, body):
        def step(i, carry):
            body(i)
            return carry

        lax.fori_loop(low, high, step, 0)

    barrier = pltpu.get_barrier_semaphore()
    each(1, n, lambda k: pl.semaphore_signal(
        barrier, inc=1, device_id=line_id(k), device_id_type=MESH))
    each(1, plane, lambda k: pl.semaphore_signal(
        barrier, inc=1, device_id=plane_id(k), device_id_type=MESH))

    def own_copy(c, r):
        return pltpu.make_async_copy(
            own_rows(c, r), wbuf.at[c, depth_at(f, r), :], own_sem.at[c, r])

    def send_own(c, step):
        for r in range(parts):
            w_copy(c, f, r, step, True).start()

    pl.semaphore_wait(barrier, n - 1 + plane - 1)

    @pl.when(f < n - 1)
    def _():
        send_own(0, 1)

    @pl.when(f > 0)
    def _():
        send_own(0, -1)

    @pl.when(f == 0)
    def _():
        send_own(1, 1)

    @pl.when(f == n - 1)
    def _():
        send_own(1, -1)

    hid_copy = pltpu.make_async_copy(hid_any, hid, hid_sem)
    for c in range(2):
        for r in range(parts):
            own_copy(c, r).start()
    hid_copy.start()

    place = lax.broadcasted_iota(jnp.int32, (8, tok), 1)
    seq = lax.broadcasted_iota(jnp.int32, (8, tok), 0)
    inside = jnp.zeros((8, tok), jnp.bool_)
    start = jnp.int32(0)
    n_seq = len_ref.shape[1]
    for j in range(n_seq):
        finish = start + len_ref[0, j]
        inside = inside | ((seq == j) & (place >= start) & (place < finish))
        start = finish
    member[...] = inside.astype(jnp.float32) * mask_ref[...].astype(jnp.float32)

    def add(c, depth, first):
        def product(i, carry):
            at = pl.ds(pl.multiple_of(i * tile, tile), tile)
            part = jnp.dot(
                hid[at, depth], wbuf[c, depth, :], preferred_element_type=jnp.float32)
            acc[c, at, :] = part if first else acc[c, at, :] + part
            return carry

        lax.fori_loop(0, tok // tile, product, 0)

    def arrive(c, j, r, step):
        w_copy(c, j, r, -step, False).wait_recv()

        @pl.when((f + step >= 0) & (f + step < n))
        def _():
            w_copy(c, j, r, step, False).start()

        if by_piece:
            add(c, depth_at(j, r), False)

    for c in range(2):
        for r in range(parts):
            own_copy(c, r).wait()
        if c == 0:
            hid_copy.wait()
        if by_piece:
            add(c, pl.ds(pl.multiple_of(f * rows, rows), rows), True)

        def visit(d, c=c):
            left, right = f - d, f + d
            for r in range(parts):
                @pl.when(left >= 0)
                def _():
                    arrive(c, left, r, 1)

                @pl.when(right < n)
                def _():
                    arrive(c, right, r, -1)

            if c == 0:
                @pl.when((d == f) & (f < n - 1))
                def _():
                    send_own(1, 1)

                @pl.when((d == n - 1 - f) & (f > 0))
                def _():
                    send_own(1, -1)

        each(1, n, visit)
        if not by_piece:
            add(c, slice(None), True)
        if c == 0:
            x_copy().start()

    x_copy().wait_recv()

    def finish_rows(i, carry):
        at = pl.ds(pl.multiple_of(i * tile, tile), tile)
        projected = acc[1, at, :] + precv[at, :]
        kv_ref[at, :] = projected.astype(jnp.bfloat16)
        chosen = member[:, at].astype(jnp.bfloat16)
        rest = projected
        for _ in range(3):
            digits = rest.astype(jnp.bfloat16)
            carry += jnp.dot(chosen, digits, preferred_element_type=jnp.float32)
            rest = rest - digits.astype(jnp.float32)
        return carry

    total = lax.fori_loop(
        0, tok // tile, finish_rows, jnp.zeros((8, cw), jnp.float32)) * ro_ref[...]
    sbuf[me] = total
    each(1, plane, lambda k: s_copy(k, me).start())
    count = jnp.sum(member[...], axis=1, keepdims=True)
    each(1, plane, lambda k: s_copy(k, lax.rem(me + k, plane)).wait_recv())
    seq_sum = jnp.sum(jnp.sum(sbuf[...], axis=0), axis=1, keepdims=True)
    reward = seq_sum / jnp.sqrt(jnp.maximum(count, 1.0))

    row = lax.broadcasted_iota(jnp.int32, (8, 128), 0)
    lane = lax.broadcasted_iota(jnp.int32, (8, 128), 1)
    row_gid = jnp.full((8, 128), -1, jnp.int32)
    lane_gid = jnp.full((8, 128), -2, jnp.int32)
    for j in range(n_seq):
        row_gid = jnp.where(row == j, gid_ref[j], row_gid)
        lane_gid = jnp.where(lane == j, gid_ref[j], lane_gid)
    reward = jnp.broadcast_to(reward, (8, 128))
    zbuf[f, 0] = reward
    zbuf[f, 1] = row_gid.astype(jnp.float32)
    each(1, n, lambda k: z_copy(k, f).start())
    mine = jnp.sum(jnp.where(row == lane, reward, 0.0), axis=0, keepdims=True)
    each(1, n, lambda k: z_copy(k, lax.rem(f + k, n)).wait_recv())
    same = (zbuf[:, 1] == lane_gid.astype(jnp.float32)[None]).astype(jnp.float32)
    rewards = zbuf[:, 0]

    def over(value):
        return jnp.sum(jnp.sum(value, axis=0), axis=0, keepdims=True)

    size = jnp.maximum(over(same), 1.0)
    mean = over(same * rewards) / size
    var = over(same * (rewards - mean[None]) ** 2) / size
    adv_ref[...] = ((mine - mean) / jnp.sqrt(var + 1.0))[:, :n_seq]

    each(1, plane, lambda k: s_copy(k, me).wait_send())
    each(1, n, lambda k: z_copy(k, f).wait_send())
    x_copy().wait_send()
    for c in range(2):
        def sent(j, c=c):
            for r in range(parts):
                @pl.when((j <= f) & (f < n - 1))
                def _():
                    w_copy(c, j, r, 1, False).wait_send()

                @pl.when((j >= f) & (f > 0))
                def _():
                    w_copy(c, j, r, -1, False).wait_send()

        each(0, n, sent)


def line_kernel(
    nt, ns, parts, tile, blocks,
    hid_any, w_any, ro_any, mask_any, len_any, gid_any,
    kv_ref, adv_ref,
    ro_ref, mask_ref, len_ref, gid_ref, small_sem,
    hid, wbuf, acc, precv, hbuf, racc, rx, rret, member, gsum, robuf, vbuf, sbuf, zbuf,
    hid_sem, own_sem, wsend, wrecv, xsend, xrecv, rsend, rrecv,
    vsend, vrecv, ssend, srecv, zsend, zrecv,
    hsend, hrecv, qsend, qrecv, bsend, brecv, line_in, plane_in,
):
    n = 4
    f, t, s = lax.axis_index("fsdp"), lax.axis_index("tp"), lax.axis_index("sect")
    plane = nt * ns
    me = t * ns + s
    rows, width = w_any.shape
    cw = width // 2
    qw = cw // 2
    piece = rows // parts
    tok, depth = hid.shape
    tiles = tok // tile
    blk = tok // blocks
    share = blk // nt
    inward = jnp.where(f < 2, 1, -1)
    outward = -inward
    outer = (f == 0) | (f == n - 1)
    inner = (f == 1) | (f == n - 2)
    near_at = jnp.where(f < 2, 0, 2 * rows)
    near = pl.ds(pl.multiple_of(near_at, rows), 2 * rows)
    far = pl.ds(pl.multiple_of(2 * rows - near_at, rows), 2 * rows)
    mate = lax.div(t, 2) * 2 + (1 - lax.rem(t, 2))
    across = lax.rem(t + 2, 4)
    cross = lax.rem(mate + 2, 4)

    def plane_id(k):
        other = lax.rem(me + k, plane)
        return {"tp": lax.div(other, ns), "sect": lax.rem(other, ns)}

    def line_id(k):
        return {"fsdp": lax.rem(f + k, n)}

    def cols(q):
        side = s if q >= 2 else 1 - s
        return pl.ds(pl.multiple_of(side * cw + (q % 2) * qw, qw), qw)

    def depth_at(j, r):
        return pl.ds(pl.multiple_of(j * rows + r * piece, piece), piece)

    def block_at(j):
        return pl.ds(pl.multiple_of(j * rows, rows), rows)

    def tile_at(i):
        return pl.ds(pl.multiple_of(i * tile, tile), tile)

    def blk_at(i):
        return pl.ds(pl.multiple_of(i * blk, blk), blk)

    def share_at(i, p):
        return pl.ds(pl.multiple_of(i * blk + p * share, share), share)

    def remote(src, dst, send, recv, device):
        return pltpu.make_async_remote_copy(
            src_ref=src, dst_ref=dst, send_sem=send, recv_sem=recv,
            device_id=device, device_id_type=MESH)

    def w_copy(q, j, r, step, own=False):
        place = wbuf.at[q, depth_at(j, r), :]
        src = w_any.at[r * piece:(r + 1) * piece, cols(q)] if own else place
        toward = 0 if step is inward else 1
        return remote(src, place, wsend.at[toward, q, r, j], wrecv.at[q, r, j], {"fsdp": f + step})

    def x_copy(q, i):
        at = tile_at(i)
        return remote(acc.at[q, at], precv.at[q, at], xsend.at[q, i], xrecv.at[q, i], {"sect": 1 - s})

    def h_copy(i):
        at = share_at(i, t)
        return remote(hid.at[at, far], hbuf.at[at], hsend.at[0, i], hrecv.at[i, t], {"fsdp": f + inward})

    def h_spread(k, i):
        p = (t, t, across)[k]
        to = (mate, across, mate)[k]
        at = share_at(i, p)
        return remote(hbuf.at[at], hbuf.at[at], hsend.at[k, i], hrecv.at[i, p], {"tp": to})

    def h_recv(i, p):
        at = share_at(i, p)
        return remote(hbuf.at[at], hbuf.at[at], hsend.at[0, i], hrecv.at[i, p], {"tp": mate})

    def q_copy(i):
        at = blk_at(i)
        return remote(racc.at[0, at], rx.at[at], qsend.at[i], qrecv.at[i], {"sect": 1 - s})

    def b_copy(i):
        at = blk_at(i)
        return remote(racc.at[1, at], rret.at[at], bsend.at[i], brecv.at[i], {"fsdp": f + outward})

    def r_copy():
        return remote(ro_ref, robuf, rsend, rrecv, {"sect": 1 - s})

    def v_copy(k, slot):
        return remote(vbuf.at[slot], vbuf.at[slot], vsend.at[k], vrecv.at[slot], line_id(k))

    def s_copy(k, slot):
        return remote(sbuf.at[slot], sbuf.at[slot], ssend.at[k], srecv.at[slot], plane_id(k))

    def z_copy(k, slot):
        return remote(zbuf.at[slot], zbuf.at[slot], zsend.at[k], zrecv.at[slot], line_id(k))

    def own_copy(q):
        return pltpu.make_async_copy(
            w_any.at[:, cols(q)], wbuf.at[q, block_at(f), :], own_sem.at[q])

    def each(low, high, body):
        def step(i, carry):
            body(i)
            return carry

        lax.fori_loop(low, high, step, 0)

    def send_own(q, step):
        for r in range(parts):
            w_copy(q, f, r, step, own=True).start()

    def take(q, j, step=None, low=0, high=parts):
        for r in range(low, high):
            w_copy(q, j, r, outward).wait_recv()
            if step is not None:
                w_copy(q, j, r, step).start()

    def tell(semaphore, device):
        pl.semaphore_signal(semaphore, inc=1, device_id=device, device_id_type=MESH)

    barrier = pltpu.get_barrier_semaphore()
    beside = ({"sect": 1 - s}, {"tp": across}, {"tp": mate})
    tell(barrier, {"fsdp": f + inward})

    @pl.when(inner)
    def _():
        tell(barrier, {"fsdp": f + outward})

    for device in beside:
        tell(barrier, device)
    small = [
        pltpu.make_async_copy(src, dst, small_sem.at[i])
        for i, (src, dst) in enumerate((
            (ro_any, ro_ref), (mask_any, mask_ref), (len_any, len_ref), (gid_any, gid_ref)))
    ]
    for copy in small:
        copy.start()
    for q in (2, 3, 0, 1):
        own_copy(q).start()
    hid_copy = pltpu.make_async_copy(hid_any, hid, hid_sem)
    hid_copy.start()
    pl.semaphore_wait(barrier, jnp.where(outer, 4, 5))

    send_own(0, inward)

    @pl.when(inner)
    def _():
        send_own(0, outward)
        tell(line_in.at[0], {"fsdp": f + inward})
        tell(line_in.at[0], {"fsdp": f + outward})

    for device in beside:
        tell(plane_in.at[0], device)
    for copy in small:
        copy.wait()
    r_copy().start()

    place = lax.broadcasted_iota(jnp.int32, (8, tok), 1)
    seq = lax.broadcasted_iota(jnp.int32, (8, tok), 0)
    inside = jnp.zeros((8, tok), jnp.bool_)
    start = jnp.int32(0)
    n_seq = len_any.shape[1]
    for j in range(n_seq):
        finish = start + len_ref[0, j]
        inside = inside | ((seq == j) & (place >= start) & (place < finish))
        start = finish
    member[...] = inside.astype(jnp.float32) * mask_ref[...].astype(jnp.float32)

    def weigh():
        line = lax.broadcasted_iota(jnp.int32, (8, qw), 0)
        total = jnp.zeros((8, rows), jnp.float32)
        for q in (2, 3, 0, 1):
            if q == 0:
                r_copy().wait_recv()
            own_copy(q).wait()
            values = (ro_ref if q >= 2 else robuf)[:, (q % 2) * qw:(q % 2 + 1) * qw]
            rest = jnp.broadcast_to(values, (8, qw))
            digits = jnp.zeros((8, qw), jnp.float32)
            for k in range(3):
                digit = rest.astype(jnp.bfloat16).astype(jnp.float32)
                digits = jnp.where(line == k, digit, digits)
                rest = rest - digit
            total += lax.dot_general(
                digits.astype(jnp.bfloat16), wbuf[q, block_at(f), :],
                (((1,), (1,)), ((), ())), preferred_element_type=jnp.float32)
        total = jnp.sum(total, axis=0, keepdims=True)
        for i in range(rows // 128):
            vbuf[f, i:i + 1, :] = total[:, i * 128:(i + 1) * 128]
        pl.semaphore_wait(plane_in.at[0], 3)
        tell(plane_in.at[1], {"sect": 1 - s})
        pl.semaphore_wait(line_in.at[0], 1)

        @pl.when(inner)
        def _():
            tell(line_in.at[1], {"fsdp": f + outward})

        @pl.when(outer)
        def _():
            pl.semaphore_wait(line_in.at[1], 1)

        for k in range(1, n):
            v_copy(k, f).start()

    def gather_tokens():
        chosen = member[...].astype(jnp.bfloat16)
        step = 512 if depth % 512 == 0 else 128

        def part(i):
            at = pl.ds(pl.multiple_of(i * step, step), step)
            gsum[:, at] = jnp.dot(chosen, hid[:, at], preferred_element_type=jnp.float32)

        each(0, depth // step, part)

    def score():
        for k in range(1, n):
            v_copy(k, lax.rem(f + k, n)).wait_recv()
        total = jnp.zeros((8, 128), jnp.float32)
        for j in range(n):
            for i in range(rows // 128):
                at = j * rows + i * 128
                total += gsum[:, at:at + 128] * vbuf[j, i:i + 1, :]
        sbuf[me] = jnp.broadcast_to(jnp.sum(total, axis=1, keepdims=True), (8, 128))
        pl.semaphore_wait(plane_in.at[1], 1)
        each(1, plane, lambda k: s_copy(k, me).start())

    row = lax.broadcasted_iota(jnp.int32, (8, 128), 0)
    lane = lax.broadcasted_iota(jnp.int32, (8, 128), 1)

    def reward():
        count = jnp.sum(member[...], axis=1, keepdims=True)
        each(1, plane, lambda k: s_copy(k, lax.rem(me + k, plane)).wait_recv())
        seq_sum = jnp.sum(sbuf[...], axis=0)
        row_gid = jnp.full((8, 128), -1, jnp.int32)
        for j in range(n_seq):
            row_gid = jnp.where(row == j, gid_ref[j], row_gid)
        zbuf[f, 0] = seq_sum / jnp.sqrt(jnp.maximum(count, 1.0))
        zbuf[f, 1] = row_gid.astype(jnp.float32)
        each(1, n, lambda k: z_copy(k, f).start())

    def advantage():
        each(1, n, lambda k: z_copy(k, lax.rem(f + k, n)).wait_recv())
        lane_gid = jnp.full((8, 128), -2, jnp.int32)
        for j in range(n_seq):
            lane_gid = jnp.where(lane == j, gid_ref[j], lane_gid)
        mine = jnp.sum(jnp.where(row == lane, zbuf[f, 0], 0.0), axis=0, keepdims=True)
        same = (zbuf[:, 1] == lane_gid.astype(jnp.float32)[None]).astype(jnp.float32)
        rewards = zbuf[:, 0]

        def over(value):
            return jnp.sum(jnp.sum(value, axis=0), axis=0, keepdims=True)

        size = jnp.maximum(over(same), 1.0)
        mean = over(same * rewards) / size
        var = over(same * (rewards - mean[None]) ** 2) / size
        adv_ref[...] = ((mine - mean) / jnp.sqrt(var + 1.0))[:, :n_seq]

    def add(q, at_depth, first=False, send=False, low=0, high=tiles):
        def product(i):
            at = tile_at(i)
            part = jnp.dot(
                hid[at, at_depth], wbuf[q, at_depth, :], preferred_element_type=jnp.float32)
            acc[q, at, :] = part if first else acc[q, at, :] + part
            if send:
                x_copy(q, i).start()

        each(low, high, product)

    whole = slice(None)

    def out_at(q):
        return slice((q - 2) * qw, (q - 1) * qw)

    def finish(q, at_depth):
        def product(i):
            at = tile_at(i)
            x_copy(q - 2, i).wait_recv()
            part = jnp.dot(
                hid[at, at_depth], wbuf[q, at_depth, :], preferred_element_type=jnp.float32)
            kv_ref[at, out_at(q)] = (acc[q, at, :] + precv[q - 2, at, :] + part).astype(jnp.bfloat16)

        each(0, tiles, product)

    def spread(i):
        h_recv(i, t).wait_recv()
        h_spread(0, i).start()
        h_spread(1, i).start()

    def relay(i):
        h_recv(i, across).wait_recv()
        h_spread(2, i).start()

    def partial(i):
        h_recv(i, mate).wait_recv()
        h_recv(i, cross).wait_recv()
        at = blk_at(i)
        racc[0, at, :] = jnp.dot(hbuf[at, :], wbuf[0, far, :], preferred_element_type=jnp.float32)
        q_copy(i).start()

    def give_back(i):
        at = blk_at(i)
        part = jnp.dot(hbuf[at, :], wbuf[2, far, :], preferred_element_type=jnp.float32)
        q_copy(i).wait_recv()
        racc[1, at, :] = part + rx[at, :]
        b_copy(i).start()

    def returned(i):
        at = blk_at(i)
        b_copy(i).wait_recv()
        kv_ref[at, out_at(2)] = (acc[2, at, :] + precv[0, at, :] + rret[at, :]).astype(jnp.bfloat16)

    @pl.when(outer)
    def _():
        send_own(1, inward)

    @pl.when(inner)
    def _():
        send_own(1, outward)

    weigh()

    @pl.when(outer)
    def _():
        mid, away, end = f + inward, f + 2 * inward, f + 3 * inward
        send_own(2, inward)
        hid_copy.wait()
        each(0, 5, lambda i: h_copy(i).start())
        for r in range(parts):
            w_copy(3, f, r, inward, own=True).start()
            h_copy(5 + r).start()
        each(5 + parts, blocks, lambda i: h_copy(i).start())
        gather_tokens()
        take(0, mid)
        add(0, near, first=True, send=True)
        score()
        for q in range(1, 4):
            take(q, mid)
            add(q, near, first=True)
        reward()
        take(1, away)
        take(1, end)
        add(1, far, send=True)
        take(3, away)
        add(3, block_at(away))
        each(0, tiles, lambda i: x_copy(0, i).wait_recv())
        each(0, 5, returned)
        take(3, end, high=parts - 1)
        for r in range(parts - 1):
            add(3, depth_at(end, r))
        take(3, end, low=parts - 1)
        finish(3, depth_at(end, parts - 1))
        advantage()
        each(5, blocks, returned)

    @pl.when(inner)
    def _():
        edge, away, end = f + outward, f + inward, f + 2 * inward
        for q in range(2, 4):
            send_own(q, outward)
        for r in range(parts):
            take(0, edge, inward, low=r, high=r + 1)
            w_copy(1, f, r, inward, own=True).start()
        hid_copy.wait()
        gather_tokens()
        take(1, edge, inward)
        send_own(3, inward)
        take(0, away)
        take(0, end)
        score()
        add(0, whole, first=True, send=True)
        take(2, edge, inward)
        send_own(2, inward)
        take(1, away, outward)
        add(1, near, first=True)
        spread(0)
        take(1, end, outward)
        reward()
        spread(1)
        add(1, far, send=True, high=tiles // 2)
        relay(0)
        spread(2)
        partial(0)
        spread(3)
        relay(1)
        partial(1)
        take(3, away, outward)
        add(1, far, send=True, low=tiles // 2, high=tiles - 1)
        relay(2)
        spread(4)
        partial(2)
        relay(3)
        partial(3)
        take(3, edge, inward, high=1)
        add(2, near, first=True)
        relay(4)
        spread(5)
        partial(4)
        take(2, end)
        take(2, away)
        each(0, 5, give_back)
        take(3, edge, inward, low=1)
        relay(5)
        spread(6)
        partial(5)
        add(1, far, send=True, low=tiles - 1)
        take(3, end, outward, high=1)
        spread(7)
        finish(2, far)
        take(3, end, outward, low=1)
        relay(6)
        give_back(5)
        partial(6)
        relay(7)
        partial(7)
        give_back(6)
        add(3, near, first=True)
        give_back(7)
        advantage()
        finish(3, far)

    for q in range(2):
        each(0, tiles, lambda i: x_copy(q, i).wait_send())
    r_copy().wait_send()
    for k in range(1, n):
        v_copy(k, f).wait_send()
    each(1, plane, lambda k: s_copy(k, me).wait_send())
    each(1, n, lambda k: z_copy(k, f).wait_send())
    for r in range(parts):
        for q in range(4):
            w_copy(q, f, r, inward).wait_send()

    @pl.when(outer)
    def _():
        each(0, blocks, lambda i: h_copy(i).wait_send())

    @pl.when(inner)
    def _():
        for r in range(parts):
            for q in range(4):
                w_copy(q, f, r, outward).wait_send()
                w_copy(q, f + outward, r, inward).wait_send()
                if q % 2:
                    w_copy(q, f + inward, r, outward).wait_send()
                    w_copy(q, f + 2 * inward, r, outward).wait_send()

        def sent(i):
            for k in range(3):
                h_spread(k, i).wait_send()
            q_copy(i).wait_send()
            b_copy(i).wait_send()

        each(0, blocks, sent)


def solution(mesh):
    n, nt, ns = mesh.shape["fsdp"], mesh.shape["tp"], mesh.shape["sect"]

    def local(hidden, kv_weight, readout, lengths, prompt_mask, group_ids):
        tok, depth = hidden.shape
        rows, width = kv_weight.shape
        parts = max(1, min(2, rows // 256))
        cw = width // 2
        plane = nt * ns
        n_seq = lengths.shape[1]
        tile = min(256, tok)
        in_line = n == 4 and nt == 4 and ns == 2 and rows % 1024 == 0 and cw % 256 == 0 and tok % 1024 == 0
        dma = pltpu.SemaphoreType.DMA
        vmem, smem, anywhere = (
            pl.BlockSpec(memory_space=pltpu.VMEM),
            pl.BlockSpec(memory_space=pltpu.SMEM),
            pl.BlockSpec(memory_space=pl.ANY),
        )
        if in_line:
            blocks = 8
            body = functools.partial(line_kernel, nt, ns, parts, tile, blocks)
            tiles = tok // tile
            qw = cw // 2
            specs = [anywhere] * 6
            scratch = [
                pltpu.VMEM((1, cw), jnp.float32),
                pltpu.VMEM((1, tok), jnp.int32),
                pltpu.SMEM((1, n_seq), jnp.int32),
                pltpu.SMEM((n_seq,), jnp.int32),
                dma((4,)),
                pltpu.VMEM((tok, depth), jnp.bfloat16),
                pltpu.VMEM((4, depth, qw), jnp.bfloat16),
                pltpu.VMEM((4, tok, qw), jnp.float32),
                pltpu.VMEM((2, tok, qw), jnp.float32),
                pltpu.VMEM((tok, 2 * rows), jnp.bfloat16),
                pltpu.VMEM((2, tok, qw), jnp.float32),
                pltpu.VMEM((tok, qw), jnp.float32),
                pltpu.VMEM((tok, qw), jnp.float32),
                pltpu.VMEM((8, tok), jnp.float32),
                pltpu.VMEM((8, depth), jnp.float32),
                pltpu.VMEM((1, cw), jnp.float32),
                pltpu.VMEM((n, rows // 128, 128), jnp.float32),
                pltpu.VMEM((plane, 8, 128), jnp.float32),
                pltpu.VMEM((n, 2, 8, 128), jnp.float32),
                dma, dma((4,)),
                dma((2, 4, parts, n)), dma((4, parts, n)),
                dma((2, tiles)), dma((2, tiles)),
                dma, dma,
                dma((n,)), dma((n,)),
                dma((plane,)), dma((plane,)),
                dma((n,)), dma((n,)),
                dma((3, blocks)), dma((blocks, nt)),
                dma((blocks,)), dma((blocks,)),
                dma((blocks,)), dma((blocks,)),
                pltpu.SemaphoreType.REGULAR((2,)), pltpu.SemaphoreType.REGULAR((2,)),
            ]
        else:
            body = functools.partial(kernel, n, nt, ns, parts, tile)
            specs = [anywhere, anywhere, vmem, vmem, smem, smem]
            scratch = [
                pltpu.VMEM((tok, depth), jnp.bfloat16),
                pltpu.VMEM((2, depth, cw), jnp.bfloat16),
                pltpu.VMEM((2, tok, cw), jnp.float32),
                pltpu.VMEM((tok, cw), jnp.float32),
                pltpu.VMEM((8, tok), jnp.float32),
                pltpu.VMEM((plane, 8, cw), jnp.float32),
                pltpu.VMEM((n, 2, 8, 128), jnp.float32),
                dma, dma((2, parts)),
                dma((2, 2, parts, n)), dma((2, parts, n)),
                dma, dma,
                dma((plane,)), dma((plane,)),
                dma((n,)), dma((n,)),
            ]
        kv, adv = pl.pallas_call(
            body,
            out_shape=(
                pltpu.VMEM((tok, width // 2), jnp.bfloat16),
                pltpu.VMEM((1, n_seq), jnp.float32),
            ),
            in_specs=specs,
            out_specs=(vmem, vmem),
            scratch_shapes=scratch,
            compiler_params=pltpu.CompilerParams(collective_id=0, has_side_effects=True),
        )(hidden, kv_weight, readout[None, :], prompt_mask[None, :], lengths, group_ids)
        return kv, adv[0]

    return jax.shard_map(
        local,
        mesh=mesh,
        in_specs=(
            P("fsdp", "sect"),
            P(("sect", "fsdp"), "tp"),
            P(("tp", "sect")),
            P("fsdp", None),
            P("fsdp"),
            P("fsdp"),
        ),
        out_specs=(P("fsdp", ("tp", "sect")), P("fsdp")),
        check_vma=False,
    )
```
